32 devices in a mesh: sec: 4 (over y, core), grp: 8 (over z, x).
Axes of the slice: x: 2, y: 2, z: 4, core: 2. Of those that a mesh axis runs over, the one named last changes fastest.
Arguments:
- solution_in: float32 [2, 32, 4, 6144], P(None, 'grp', None, 'sec'), may hold values from -6 to 6
- residual_in: float32 [2, 32, 4, 6144], P(None, 'grp', None, 'sec'), may hold values from -6 to 6
- direction_in: float32 [2, 32, 4, 6144], P(None, 'grp', None, 'sec'), may hold values from -6 to 6
- legendre: bfloat16 [32, 2, 128, 6144], P('grp', None, None, 'sec'), may hold values from -0.0034179688 to 0.0034179688
- inverse_prior: float32 [2, 6144], P(None, 'sec'), may hold values from 0.3 to 10
- noise_qq: float32 [128, 8192], P('grp', 'sec'), may hold values from 0.5 to 4
- noise_qu: float32 [128, 8192], P('grp', 'sec'), may hold values from -0.3 to 0.3
- noise_uu: float32 [128, 8192], P('grp', 'sec'), may hold values from 0.5 to 4
- pixel_mask: int32 [128, 8192], P('grp', 'sec'), may hold values 0 or 1
- cycle_phase: float32 [128], replicated, as said below
- m_values: int32 [32], replicated, may hold values from 0 to 6143, as said below
Outputs:
- solution: float32 [2, 32, 4, 6144], P(None, 'grp', None, 'sec')
- residual: float32 [2, 32, 4, 6144], P(None, 'grp', None, 'sec')
- direction: float32 [2, 32, 4, 6144], P(None, 'grp', None, 'sec')
The draws below stay inside these ranges and needn't reach their ends.
Inputs may be any that keep to these rules, and one draw needn't show every extreme that they name: `m_values`: the slots' m values are distinct, and exactly one slot has m = 0. `cycle_phase`: each phase lies between 0 and 2 pi / 8192.
All inputs are finite; a program needn't handle non-finite values. No bound on the sum of `pixel_mask` on one device may be relied on, other than what follows from the above.
Results may differ from the reference program's by a relative error of at most 0.025.
Values sent between devices are 32-bit elements; how exact they have to be, the bound alone decides.
No kernel may reach another device: no remote copies, remote signals or barrier semaphores. Data moves between devices by JAX's collectives and lax.ppermute only.
A program may use at most 64 MiB of HBM per device.

```python
import math
import jax
import jax.numpy as jnp
from jax import lax

L = 6144
NPHI = 8192
ITERS = 4
M = 32
CYCLES = 128


def draw_cycle_phase(key, part):
    uniform_values = jax.random.uniform(jax.random.fold_in(key, 11), (CYCLES,), jnp.float32)
    return (uniform_values * (2.0 * math.pi / NPHI)).astype(jnp.float32)


def draw_m_values(key, part):
    order = jax.random.permutation(jax.random.fold_in(key, 23), L - 1)
    chosen = order[:M].astype(jnp.int32) + 1
    zero_slot = jax.random.randint(jax.random.fold_in(key, 29), (), 0, M, dtype=jnp.int32)
    slots = jnp.arange(M, dtype=jnp.int32)
    return jnp.where(slots == zero_slot, 0, chosen).astype(jnp.int32)


def touch_ends(array, own_key, least, high):
    longest = array.shape.index(max(array.shape))
    spots = []
    for shift in (0, 1):
        where = [jax.random.randint(jax.random.fold_in(own_key, axis), (), 0, length) for axis, length in enumerate(array.shape)]
        where[longest] = (where[longest] + shift) % array.shape[longest]
        spots.append(tuple(where))
    return array.at[spots[0]].set(least).at[spots[1]].set(high)


def level_of(key, extent, split, low, largest):
    factor_of, own = 1.0, jax.random.fold_in(key, 6)
    for position, shards_of in split:
        heights = jnp.exp(jax.random.uniform(jax.random.fold_in(own, position), (shards_of,), jnp.float32, low / len(split), largest / len(split)))
        factor_of = factor_of * jnp.repeat(heights, extent[position] // shards_of).reshape([-1 if axis == position else 1 for axis in range(len(extent))])
    return factor_of


def noise(key, dims, width, reach, pieces=(), held_as=jnp.bfloat16):
    factor_of = level_of(key, dims, pieces, -0.22, 0.18) if pieces else 1.0
    values = jax.random.normal(key, dims, jnp.float32) * width * factor_of
    return jnp.minimum(jnp.maximum(values, -reach), reach).astype(held_as)


def setup_inputs(seed: int = 0) -> dict:
    key_list = jax.random.split(jax.random.key(seed), 12)
    solution_in = noise(key_list[0], (2, M, 4, L), 1.0, 6.0, ((1, 8), (3, 4)), jnp.float32)
    residual_in = noise(key_list[1], (2, M, 4, L), 1.0, 6.0, ((1, 8), (3, 4)), jnp.float32)
    direction_in = noise(key_list[2], (2, M, 4, L), 1.0, 6.0, ((1, 8), (3, 4)), jnp.float32)
    legendre = noise(key_list[3], (M, 2, CYCLES, L), (16 * L * M) ** -0.5, 0.0034179688, ((0, 8), (3, 4)))
    inverse_prior = jnp.clip(jnp.exp(math.log(10.0) - 3.506558 * jax.random.uniform(key_list[4], (2, L), jnp.float32) ** level_of(key_list[4], (2, L), ((1, 4),), -0.2, 0.2)), 0.3, 10.0)
    noise_qq = jnp.clip(jnp.exp(math.log(4.0) - 2.0794415 * jax.random.uniform(key_list[5], (CYCLES, NPHI), jnp.float32) ** level_of(key_list[5], (CYCLES, NPHI), ((0, 8), (1, 4)), -0.2, 0.2)), 0.5, 4.0)
    noise_qu = jnp.clip(jax.random.uniform(key_list[6], (CYCLES, NPHI), jnp.float32, -0.3, 0.3) * level_of(key_list[6], (CYCLES, NPHI), ((0, 8), (1, 4)), -0.4, 0.0), -0.3, 0.3)
    noise_uu = jnp.clip(jnp.exp(math.log(4.0) - 2.0794415 * jax.random.uniform(key_list[7], (CYCLES, NPHI), jnp.float32) ** level_of(key_list[7], (CYCLES, NPHI), ((0, 8), (1, 4)), -0.2, 0.2)), 0.5, 4.0)
    pixel_mask = touch_ends((jax.random.randint(key_list[8], (CYCLES, NPHI), 0, 4) < 3).astype(jnp.int32), jax.random.fold_in(key_list[8], 1), 0, 1)
    cycle_phase = draw_cycle_phase(jax.random.fold_in(key_list[11], 71), 0)
    m_values = draw_m_values(jax.random.fold_in(key_list[11], 71), 0)
    return {"solution_in": solution_in, "residual_in": residual_in, "direction_in": direction_in, "legendre": legendre, "inverse_prior": inverse_prior, "noise_qq": noise_qq, "noise_qu": noise_qu, "noise_uu": noise_uu, "pixel_mask": pixel_mask, "cycle_phase": cycle_phase, "m_values": m_values}


full_turn = 2.0 * math.pi


def combine_modes(prod):
    plus = prod[:, :, 0]
    minus = prod[:, :, 1]
    return jnp.stack([-plus[:, :, 0] + minus[:, :, 3], -plus[:, :, 1] - minus[:, :, 2],
                      -plus[:, :, 2] - minus[:, :, 1], -plus[:, :, 3] + minus[:, :, 0]], axis=2)


def adjoint_terms(field):
    half = field.astype(jnp.bfloat16)
    minus_part = jnp.stack([half[:, :, 3], -half[:, :, 2], -half[:, :, 1], half[:, :, 0]], axis=2)
    return jnp.stack([-half, minus_part], axis=2)


def legendre_forward(coeffs, legendre):
    half = coeffs.astype(jnp.bfloat16).astype(jnp.float32)

    def single(item):
        values, table = item
        return jnp.einsum('srl,bcl->bscr', table.astype(jnp.float32), values, precision=lax.Precision.HIGHEST)

    prod = lax.map(single, (half.transpose(1, 0, 2, 3), legendre))
    return combine_modes(prod.transpose(1, 0, 2, 3, 4))


def legendre_adjoint(field, legendre):
    both = adjoint_terms(field).astype(jnp.float32)

    def single(item):
        values, table = item
        return jnp.einsum('srl,bscr->bcl', table.astype(jnp.float32), values, precision=lax.Precision.HIGHEST)

    out = lax.map(single, (both.transpose(1, 0, 2, 3, 4), legendre))
    return out.transpose(1, 0, 2, 3)


def phi_table(m_values, start, count, total):
    index = start + jnp.arange(count, dtype=jnp.int32)
    folded = (m_values[:, None] * index[None, :]) % total
    angle = folded.astype(jnp.float32) * (full_turn / total)
    weight = jnp.where(m_values == 0, 1.0, 2.0).astype(jnp.float32)[:, None]
    return jnp.concatenate([weight * jnp.cos(angle), -weight * jnp.sin(angle)], axis=0)


def pixel_segment(field, cosines, sine_table, table, noise_qq, noise_qu, noise_uu, mask_f):
    count = field.shape[0]
    modes = field.shape[1]
    cycles = field.shape[3]
    parts = field.reshape(count, modes, 2, 2, cycles)
    real = parts[:, :, :, 0]
    imag = parts[:, :, :, 1]
    cosm = cosines[None, :, None, :]
    sinm = sine_table[None, :, None, :]
    rot_re = real * cosm - imag * sinm
    rot_im = real * sinm + imag * cosm
    rows = jnp.stack([rot_re, rot_im], axis=1).transpose(0, 3, 4, 1, 2).reshape(count * 2 * cycles, 2 * modes)
    pixels = jnp.dot(rows, table, precision=lax.Precision.HIGHEST, preferred_element_type=jnp.float32)
    pixels = pixels.reshape(count, 2, cycles, -1)
    qpart = pixels[:, 0]
    upart = pixels[:, 1]
    wq = mask_f * (noise_qq * qpart + noise_qu * upart)
    wu = mask_f * (noise_qu * qpart + noise_uu * upart)
    weighted = jnp.stack([wq, wu], axis=1).reshape(count * 2 * cycles, -1)
    back = jnp.dot(weighted, table.T, precision=lax.Precision.HIGHEST, preferred_element_type=jnp.float32)
    back = back.reshape(count, 2, cycles, 2, modes)
    kernel_real = back[:, :, :, 0]
    kernel_imaginary = back[:, :, :, 1]
    cosine_theta = cosines.T[None, None]
    sine_theta = sine_table.T[None, None]
    gathered_real = kernel_real * cosine_theta + kernel_imaginary * sine_theta
    gathered_imaginary = kernel_imaginary * cosine_theta - kernel_real * sine_theta
    out = jnp.stack([gathered_real, gathered_imaginary], axis=2)
    return out.transpose(0, 4, 1, 2, 3).reshape(count, modes, 4, cycles)


def totals(values):
    return jnp.sum(values, axis=(1, 2, 3))


def reference(solution_in, residual_in, direction_in, legendre, inverse_prior, noise_qq, noise_qu, noise_uu, pixel_mask, cycle_phase, m_values):
    table = phi_table(m_values, 0, NPHI, NPHI)
    angle = m_values.astype(jnp.float32)[:, None] * cycle_phase[None, :]
    cosines = jnp.cos(angle)
    sine_table = jnp.sin(angle)
    mask_f = pixel_mask.astype(jnp.float32)
    prior = jnp.repeat(inverse_prior, 2, axis=0)[None, None]

    def apply(vector):
        field = legendre_forward(vector, legendre)
        folded = pixel_segment(field, cosines, sine_table, table, noise_qq, noise_qu, noise_uu, mask_f)
        return prior * vector + legendre_adjoint(folded, legendre)

    solution, residual, direction = solution_in, residual_in, direction_in
    norm_now = totals(residual * residual)
    for step in range(ITERS):
        image = apply(direction)
        alpha = (norm_now / totals(direction * image))[:, None, None, None]
        solution = solution + alpha * direction
        residual = residual - alpha * image
        norm_next = totals(residual * residual)
        direction = residual + (norm_next / norm_now)[:, None, None, None] * direction
        norm_now = norm_next
    return solution, residual, direction
```

```python
import functools
import math

import jax
import jax.numpy as jnp
from jax import lax
from jax.experimental import pallas as pl
from jax.experimental.pallas import tpu as pltpu
from jax.sharding import PartitionSpec as P

ITERS = 4
LANES = 128
ROWS = 8
full_turn = 2.0 * math.pi
f32 = jnp.float32
bf16 = jnp.bfloat16

to_message = tuple(b * 4 + p * 2 + q for q in (0, 1) for b in (0, 1) for p in (0, 1))
from_message = tuple(to_message.index(n) for n in range(ROWS))
flipped = tuple(n ^ 3 for n in range(ROWS))


def row_index(shape):
    return lax.broadcasted_iota(jnp.int32, shape, 0)


def lane_index(shape):
    return lax.broadcasted_iota(jnp.int32, shape, 1)


def permute_rows(x, order):
    rows = row_index(x.shape)
    by_shift = {}
    for t, n in enumerate(order):
        by_shift.setdefault((t - n) % ROWS, []).append(t)
    out = None
    for shift, targets in by_shift.items():
        moved = pltpu.roll(x, shift, 0) if shift else x
        if out is None:
            out = moved
        else:
            mask = functools.reduce(jnp.logical_or, [rows == t for t in targets])
            out = jnp.where(mask, moved, out)
    return out


def swap_blocks(x):
    width = LANES // ROWS
    rows = row_index(x.shape)
    block = lane_index(x.shape) // width
    for k in (4, 2, 1):
        row_bit = (rows & k) != 0
        block_bit = (block & k) != 0
        down = pltpu.roll(pltpu.roll(x, k, 0), (LANES - k * width) % LANES, 1)
        if k == 4:
            x = jnp.where(row_bit != block_bit, down, x)
        else:
            up = pltpu.roll(pltpu.roll(x, ROWS - k, 0), k * width, 1)
            x = jnp.where(row_bit == block_bit, x, jnp.where(row_bit, down, up))
    return x


def split_rows(x):
    high = x.astype(bf16).astype(f32)
    return jnp.concatenate([high, x - high], axis=0).astype(bf16)


def flip_signed(x):
    rows = row_index(x.shape)
    same = ((rows >> 1) & 1) == (rows & 1)
    moved = permute_rows(x, flipped)
    return jnp.where(same, moved, -moved)


def row_totals(x):
    tile = x[:, :LANES]
    for k in range(1, x.shape[1] // LANES):
        tile = tile + x[:, k * LANES : (k + 1) * LANES]
    rows = row_index(tile.shape)
    first = jnp.sum(jnp.where(rows < 4, tile, 0.0), axis=0, keepdims=True)
    second = jnp.sum(jnp.where(rows < 4, 0.0, tile), axis=0, keepdims=True)
    return join_halves(first, second)


def join_halves(first, second):
    first = first + pltpu.roll(first, LANES // 2, 1)
    second = second + pltpu.roll(second, LANES // 2, 1)
    return jnp.where(lane_index(first.shape) < LANES // 2, first, second)


def pair(vector):
    low = lane_index(vector.shape) < LANES // 2
    return (
        jnp.sum(jnp.where(low, vector, 0.0), axis=1, keepdims=True),
        jnp.sum(jnp.where(low, 0.0, vector), axis=1, keepdims=True),
    )


def by_row(two, shape):
    return jnp.where(row_index(shape) < 4, two[0], two[1])


def by_lane(two, shape):
    quarter = LANES // 4
    return jnp.where((lane_index(shape) // quarter) % 2 == 0, two[0], two[1])


def forward_send(values, legendre_ref, send_ref, m, sections, cycles):
    prod = lax.dot_general(
        split_rows(values),
        legendre_ref[m],
        (((1,), (1,)), ((), ())),
        preferred_element_type=f32,
    )
    prod = prod[:ROWS] + prod[ROWS:]
    field = flip_signed(prod[:, cycles:]) - prod[:, :cycles]
    field = permute_rows(field, to_message)
    groups = send_ref.shape[0] // sections
    for k in range(cycles // LANES):
        tile = swap_blocks(field[:, k * LANES : (k + 1) * LANES])
        for s in range(sections):
            start = s * groups + k * ROWS
            send_ref[start : start + ROWS, 0, m * LANES : (m + 1) * LANES] = tile


def send_scalars(send_ref, vector, slots):
    count = send_ref.shape[0]
    send_ref[:, 0, slots * LANES :] = jnp.broadcast_to(vector, (count, LANES))


def received_scalars(recv_ref, slots):
    return jnp.sum(recv_ref[:, 0, slots * LANES :], axis=0, keepdims=True)


def received_tile(recv_ref, m, k, sections):
    groups = recv_ref.shape[0] // sections
    total = None
    for s in range(sections):
        start = s * groups + k * ROWS
        part = recv_ref[start : start + ROWS, 0, m * LANES : (m + 1) * LANES]
        total = part if total is None else total + part
    return total


def start_kernel(sections, cycles, residual_ref, direction_ref, legendre_ref, send_ref, r_ref, d_ref):
    slots = r_ref.shape[0]
    square = None
    for m in range(slots):
        r = jnp.concatenate([residual_ref[0, m], residual_ref[1, m]], axis=0)
        d = jnp.concatenate([direction_ref[0, m], direction_ref[1, m]], axis=0)
        r_ref[m] = r
        d_ref[m] = d
        square = r * r if square is None else square + r * r
        forward_send(d, legendre_ref, send_ref, m, sections, cycles)
    send_scalars(send_ref, row_totals(square), slots)


def table_kernel(
    slots, m_ref, phase_ref, qq_ref, qu_ref, uu_ref, mask_ref, table_ref, cos_ref, sin_ref, nqq_ref, nqu_ref, nuu_ref
):
    total_m = cos_ref.shape[0]
    count = nqq_ref.shape[1]
    total = count * lax.axis_size("sec")
    groups = total_m // slots
    rows = row_index((ROWS, LANES))
    columns = []
    for m in range(slots):
        for k in range(groups // ROWS):
            column = jnp.zeros((ROWS, LANES), jnp.int32)
            for i in range(ROWS):
                column = jnp.where(rows == i, m_ref[(k * ROWS + i) * slots + m], column)
            columns.append(column)
    column = jnp.concatenate(columns, axis=0)
    value = column.astype(f32)
    weight = jnp.where(column == 0, 1.0, 2.0).astype(f32)
    lanes = lane_index(column.shape)

    me = lax.axis_index("grp")
    width = LANES // ROWS
    phases = phase_ref[pl.ds(me // ROWS, 1), :]
    spot = lane_index(phases.shape)
    moved = pltpu.roll(phases, (ROWS - me % ROWS) % ROWS * width, 1)
    local = jnp.where(spot < width, moved, 0.0)
    for k in (1, 2, 4):
        local = local + pltpu.roll(local, k * width, 1)
    turn = value * local
    cosine = jnp.cos(turn)
    sine = jnp.sin(turn)
    cos_ref[...] = cosine
    sin_ref[...] = jnp.where(lanes < LANES // 2, -sine, sine)

    def wrap(index):
        return index & (total - 1) if total & (total - 1) == 0 else index % total

    step = full_turn / total
    start = lax.axis_index("sec") * count
    fine = wrap(column * lanes).astype(f32) * step
    coarse = wrap(column * (start + lanes * LANES)).astype(f32) * step
    fine_cos, fine_sin = jnp.cos(fine), jnp.sin(fine)
    coarse_cos, coarse_sin = weight * jnp.cos(coarse), weight * jnp.sin(coarse)
    for a in range(count // LANES):
        cos_a = coarse_cos[:, a : a + 1]
        sin_a = coarse_sin[:, a : a + 1]
        block = jnp.concatenate([cos_a * fine_cos - sin_a * fine_sin, -(sin_a * fine_cos + cos_a * fine_sin)], axis=0)
        high = block.astype(bf16)
        low = (block - high.astype(f32)).astype(bf16)
        here = slice(a * LANES, (a + 1) * LANES)
        table_ref[: 2 * total_m, here] = high
        table_ref[2 * total_m : 4 * total_m, here] = low
        table_ref[4 * total_m :, here] = high
    mask = mask_ref[...].astype(f32)
    nqq_ref[...] = mask * qq_ref[...]
    nqu_ref[...] = mask * qu_ref[...]
    nuu_ref[...] = mask * uu_ref[...]


def pixel_kernel(
    sections,
    chunk,
    first,
    recv_ref,
    table_ref,
    cos_ref,
    sin_ref,
    nqq_ref,
    nqu_ref,
    nuu_ref,
    prior_ref,
    r_ref,
    d_ref,
    field_ref,
    rr_ref,
    send_ref,
    field_out,
    rr_out,
    d_out,
):
    total_m = cos_ref.shape[0]
    slots = r_ref.shape[0]
    groups = total_m // slots
    tiles = [received_tile(recv_ref, m, k, sections) for m in range(slots) for k in range(groups // ROWS)]
    field = jnp.concatenate(tiles, axis=0)
    scalars = received_scalars(recv_ref, slots)
    rr_out[...] = scalars
    if not first:
        now, before = pair(scalars), pair(rr_ref[...])
        ratio = tuple(a / b for a, b in zip(now, before))
        field = field + by_lane(ratio, field.shape) * field_ref[...]
    field_out[...] = field
    half = LANES // 2
    cosine, sine = cos_ref[...], sin_ref[...]
    turned = field * cosine + pltpu.roll(field, half, 1) * sine
    modes = jnp.concatenate([turned[:, :half], turned[:, half:]], axis=0)
    high = modes.astype(bf16).astype(f32)
    rows3 = jnp.concatenate([high, high, modes - high], axis=0).astype(bf16)
    count = nqq_ref.shape[1]
    cycles = nqq_ref.shape[0]
    back = None
    curve = [None, None]
    for c in range(count // chunk):
        here = slice(c * chunk, (c + 1) * chunk)
        pixels = lax.dot_general(
            rows3, table_ref[:, here], (((0,), (0,)), ((), ())), preferred_element_type=f32
        )
        nqq, nqu, nuu = nqq_ref[:, here], nqu_ref[:, here], nuu_ref[:, here]
        parts = []
        for b in range(2):
            q = pixels[2 * b * cycles : (2 * b + 1) * cycles]
            u = pixels[(2 * b + 1) * cycles : (2 * b + 2) * cycles]
            wq = nqq * q + nqu * u
            wu = nqu * q + nuu * u
            parts += [wq, wu]
            product = wq * q + wu * u
            curve[b] = product if curve[b] is None else curve[b] + product
        weighted = jnp.concatenate(parts, axis=0)
        high = weighted.astype(bf16).astype(f32)
        both = jnp.concatenate([high, weighted - high], axis=0).astype(bf16)
        part = lax.dot_general(
            table_ref[: 4 * total_m, here], both, (((1,), (1,)), ((), ())), preferred_element_type=f32
        )
        back = part if back is None else back + part
    top = 2 * total_m
    folded = back[:top, :half] + (back[:top, half:] + back[top:, :half])
    folded = jnp.concatenate([folded[:total_m], folded[total_m:]], axis=1)
    out = folded * cosine - pltpu.roll(folded, half, 1) * sine
    for m in range(slots):
        for k in range(groups // ROWS):
            at = (m * (groups // ROWS) + k) * ROWS
            for s in range(sections):
                start = s * groups + k * ROWS
                send_ref[start : start + ROWS, 0, m * LANES : (m + 1) * LANES] = out[at : at + ROWS]

    prior = prior_rows(prior_ref)
    own = None
    for m in range(slots):
        d = d_ref[m]
        if not first:
            d = r_ref[m] + by_row(ratio, (ROWS, LANES))[:, :1] * d
        d_out[m] = d
        product = prior * d * d
        own = product if own is None else own + product

    def fold(x):
        x = jnp.sum(x, axis=0, keepdims=True)
        tile = x[:, :LANES]
        for k in range(1, x.shape[1] // LANES):
            tile = tile + x[:, k * LANES : (k + 1) * LANES]
        return tile

    send_scalars(send_ref, join_halves(fold(curve[0]), fold(curve[1])) + row_totals(own), slots)


def prior_rows(prior_ref):
    e = prior_ref[0:1, :]
    b = prior_ref[1:2, :]
    shape = (ROWS, prior_ref.shape[1])
    return jnp.where((row_index(shape) >> 1) & 1 == 0, jnp.broadcast_to(e, shape), jnp.broadcast_to(b, shape))


def image_step(sections, cycles, recv_ref, rr_ref, prior_ref, legendre_ref, r_ref, d_ref, m, alpha, prior):
    tiles = []
    for k in range(cycles // LANES):
        tiles.append(permute_rows(swap_blocks(received_tile(recv_ref, m, k, sections)), from_message))
    field = jnp.concatenate(tiles, axis=1) if len(tiles) > 1 else tiles[0]
    both = split_rows(jnp.concatenate([-field, flip_signed(field)], axis=1))
    image = jnp.dot(both, legendre_ref[m], preferred_element_type=f32)
    image = (image[:ROWS] + image[ROWS:]) + prior * d_ref[m]
    return r_ref[m] - alpha * image


def step_size(recv_ref, rr_ref, slots):
    curve = pair(received_scalars(recv_ref, slots))
    two = tuple(a / b for a, b in zip(pair(rr_ref[...]), curve))
    return by_row(two, (ROWS, LANES))[:, :1]


def update_kernel(
    sections, cycles, first, recv_ref, rr_ref, prior_ref, legendre_ref, r_ref, d_ref, x_ref, send_ref, r_out, x_out
):
    slots = r_ref.shape[0]
    alpha = step_size(recv_ref, rr_ref, slots)
    prior = prior_rows(prior_ref)
    square = None
    for m in range(slots):
        r = image_step(sections, cycles, recv_ref, rr_ref, prior_ref, legendre_ref, r_ref, d_ref, m, alpha, prior)
        r_out[m] = r
        square = r * r if square is None else square + r * r
        forward_send(r, legendre_ref, send_ref, m, sections, cycles)
        x_out[m] = alpha * d_ref[m] if first else x_ref[m] + alpha * d_ref[m]
    send_scalars(send_ref, row_totals(square), slots)


def last_kernel(
    sections,
    cycles,
    recv_ref,
    rr_ref,
    prior_ref,
    legendre_ref,
    r_ref,
    d_ref,
    x_ref,
    solution_ref,
    send_ref,
    residual_out,
    solution_out,
):
    slots = r_ref.shape[0]
    alpha = step_size(recv_ref, rr_ref, slots)
    prior = prior_rows(prior_ref)
    square = None
    for m in range(slots):
        r = image_step(sections, cycles, recv_ref, rr_ref, prior_ref, legendre_ref, r_ref, d_ref, m, alpha, prior)
        square = r * r if square is None else square + r * r
        x = x_ref[m] + alpha * d_ref[m]
        for b in range(2):
            residual_out[b, m] = r[4 * b : 4 * b + 4]
            solution_out[b, m] = solution_ref[b, m] + x[4 * b : 4 * b + 4]
    send_scalars(send_ref, row_totals(square), 0)


def end_kernel(recv_ref, rr_ref, d_ref, residual_ref, direction_out):
    slots = d_ref.shape[0]
    now, before = pair(received_scalars(recv_ref, 0)), pair(rr_ref[...])
    for b in range(2):
        ratio = now[b] / before[b]
        for m in range(slots):
            direction_out[b, m] = residual_ref[b, m] + ratio * d_ref[m, 4 * b : 4 * b + 4]


def call(kernel, outs, name, limit=32 << 20, smem=()):
    def run(*args):
        vmem = pl.BlockSpec(memory_space=pltpu.VMEM)
        specs = [pl.BlockSpec(memory_space=pltpu.SMEM) if i in smem else vmem for i in range(len(args))]
        return pl.pallas_call(
            kernel,
            out_shape=[jax.ShapeDtypeStruct(shape, dtype) for shape, dtype in outs],
            in_specs=specs,
            out_specs=[vmem] * len(outs),
            compiler_params=pltpu.CompilerParams(vmem_limit_bytes=limit),
            name=name,
        )(*args)

    return run


def per_device(
    solution_in,
    residual_in,
    direction_in,
    legendre,
    inverse_prior,
    noise_qq,
    noise_qu,
    noise_uu,
    pixel_mask,
    cycle_phase,
    m_values,
):
    sections = lax.axis_size("sec")
    devices = sections * lax.axis_size("grp")
    slots, cycles, length = legendre.shape[0], legendre.shape[2], legendre.shape[3]
    total_m = m_values.shape[0]
    count = noise_qq.shape[1]
    table = legendre.reshape(slots, 2 * cycles, length)
    message = ((devices, 1, (slots + 1) * LANES), f32)
    scalars = ((devices, 1, LANES), f32)
    inner = ((slots, ROWS, length), f32)
    outer = (solution_in.shape, f32)
    vector = ((1, LANES), f32)
    field_like = ((total_m, LANES), f32)
    noise_like = (noise_qq.shape, f32)
    chunk = min(512, count)

    def exchange(x):
        return lax.all_to_all(x, ("sec", "grp"), 0, 0, tiled=True)

    send, r, d = call(functools.partial(start_kernel, sections, cycles), [message, inner, inner], "start")(
        residual_in, direction_in, table
    )
    trig, cosine, sine, nqq, nqu, nuu = call(
        functools.partial(table_kernel, slots),
        [((6 * total_m, count), bf16), field_like, field_like, noise_like, noise_like, noise_like],
        "tables",
        smem=(0,),
    )(m_values, cycle_phase.reshape(-1, LANES), noise_qq, noise_qu, noise_uu, pixel_mask)
    field = cosine
    rr = cosine[:1]
    x = r
    for step in range(ITERS):
        first, last = step == 0, step == ITERS - 1
        recv = exchange(send)
        send, field, rr, d = call(
            functools.partial(pixel_kernel, sections, chunk, first), [message, field_like, vector, inner], "pixels"
        )(recv, trig, cosine, sine, nqq, nqu, nuu, inverse_prior, r, d, field, rr)
        recv = exchange(send)
        if last:
            send, residual, solution = call(
                functools.partial(last_kernel, sections, cycles), [scalars, outer, outer], "last"
            )(recv, rr, inverse_prior, table, r, d, x, solution_in)
        else:
            send, r, x = call(
                functools.partial(update_kernel, sections, cycles, first), [message, inner, inner], "update"
            )(recv, rr, inverse_prior, table, r, d, x)
    recv = exchange(send)
    (direction,) = call(end_kernel, [outer], "end")(recv, rr, d, residual)
    return solution, residual, direction


def solution(mesh):
    return jax.shard_map(
        per_device,
        mesh=mesh,
        in_specs=(
            P(None, "grp", None, "sec"),
            P(None, "grp", None, "sec"),
            P(None, "grp", None, "sec"),
            P("grp", None, None, "sec"),
            P(None, "sec"),
            P("grp", "sec"),
            P("grp", "sec"),
            P("grp", "sec"),
            P("grp", "sec"),
            P(),
            P(),
        ),
        out_specs=(
            P(None, "grp", None, "sec"),
            P(None, "grp", None, "sec"),
            P(None, "grp", None, "sec"),
        ),
        check_vma=False,
    )
```

```python
import functools
import math

import jax
import jax.numpy as jnp
from jax import lax
from jax.experimental import pallas as pl
from jax.experimental.pallas import tpu as pltpu
from jax.sharding import PartitionSpec as P

ITERS = 4
LANES = 128
ROWS = 8
full_turn = 2.0 * math.pi
f32 = jnp.float32
bf16 = jnp.bfloat16

to_message = tuple(b * 4 + p * 2 + q for q in (0, 1) for b in (0, 1) for p in (0, 1))
from_message = tuple(to_message.index(n) for n in range(ROWS))
flipped = tuple(n ^ 3 for n in range(ROWS))


def row_index(shape):
    return lax.broadcasted_iota(jnp.int32, shape, 0)


def lane_index(shape):
    return lax.broadcasted_iota(jnp.int32, shape, 1)


def permute_rows(x, order):
    rows = row_index(x.shape)
    by_shift = {}
    for t, n in enumerate(order):
        by_shift.setdefault((t - n) % ROWS, []).append(t)
    out = None
    for shift, targets in by_shift.items():
        moved = pltpu.roll(x, shift, 0) if shift else x
        if out is None:
            out = moved
        else:
            mask = functools.reduce(jnp.logical_or, [rows == t for t in targets])
            out = jnp.where(mask, moved, out)
    return out


def swap_blocks(x):
    width = LANES // ROWS
    rows = row_index(x.shape)
    block = lane_index(x.shape) // width
    for k in (4, 2, 1):
        row_bit = (rows & k) != 0
        block_bit = (block & k) != 0
        down = pltpu.roll(pltpu.roll(x, k, 0), (LANES - k * width) % LANES, 1)
        if k == 4:
            x = jnp.where(row_bit != block_bit, down, x)
        else:
            up = pltpu.roll(pltpu.roll(x, ROWS - k, 0), k * width, 1)
            x = jnp.where(row_bit == block_bit, x, jnp.where(row_bit, down, up))
    return x


def split_rows(x):
    high = x.astype(bf16).astype(f32)
    return jnp.concatenate([high, x - high], axis=0).astype(bf16)


def flip_signed(x):
    rows = row_index(x.shape)
    same = ((rows >> 1) & 1) == (rows & 1)
    moved = permute_rows(x, flipped)
    return jnp.where(same, moved, -moved)


def row_totals(x):
    tile = x[:, :LANES]
    for k in range(1, x.shape[1] // LANES):
        tile = tile + x[:, k * LANES : (k + 1) * LANES]
    rows = row_index(tile.shape)
    first = jnp.sum(jnp.where(rows < 4, tile, 0.0), axis=0, keepdims=True)
    second = jnp.sum(jnp.where(rows < 4, 0.0, tile), axis=0, keepdims=True)
    return join_halves(first, second)


def join_halves(first, second):
    first = first + pltpu.roll(first, LANES // 2, 1)
    second = second + pltpu.roll(second, LANES // 2, 1)
    return jnp.where(lane_index(first.shape) < LANES // 2, first, second)


def pair(vector):
    low = lane_index(vector.shape) < LANES // 2
    return (
        jnp.sum(jnp.where(low, vector, 0.0), axis=1, keepdims=True),
        jnp.sum(jnp.where(low, 0.0, vector), axis=1, keepdims=True),
    )


def by_row(two, shape):
    return jnp.where(row_index(shape) < 4, two[0], two[1])


def by_lane(two, shape):
    quarter = LANES // 4
    return jnp.where((lane_index(shape) // quarter) % 2 == 0, two[0], two[1])


def forward_send(values, legendre_ref, send_ref, m, sections, cycles):
    prod = lax.dot_general(
        split_rows(values),
        legendre_ref[m],
        (((1,), (1,)), ((), ())),
        preferred_element_type=f32,
    )
    prod = prod[:ROWS] + prod[ROWS:]
    field = flip_signed(prod[:, cycles:]) - prod[:, :cycles]
    field = permute_rows(field, to_message)
    groups = send_ref.shape[0] // sections
    for k in range(cycles // LANES):
        tile = swap_blocks(field[:, k * LANES : (k + 1) * LANES])
        for s in range(sections):
            start = s * groups + k * ROWS
            send_ref[start : start + ROWS, 0, m * LANES : (m + 1) * LANES] = tile


def send_scalars(send_ref, vector, slots):
    count = send_ref.shape[0]
    send_ref[:, 0, slots * LANES :] = jnp.broadcast_to(vector, (count, LANES))


def received_scalars(recv_ref, slots):
    return jnp.sum(recv_ref[:, 0, slots * LANES :], axis=0, keepdims=True)


def received_tile(recv_ref, m, k, sections):
    groups = recv_ref.shape[0] // sections
    total = None
    for s in range(sections):
        start = s * groups + k * ROWS
        part = recv_ref[start : start + ROWS, 0, m * LANES : (m + 1) * LANES]
        total = part if total is None else total + part
    return total


def fill_tables(slots, total, m_ref, phase_ref, table_ref, cos_ref, sin_ref):
    total_m = cos_ref.shape[0]
    count = table_ref.shape[1]
    groups = total_m // slots
    rows = row_index((ROWS, LANES))
    columns = []
    for m in range(slots):
        for k in range(groups // ROWS):
            column = jnp.zeros((ROWS, LANES), jnp.int32)
            for i in range(ROWS):
                column = jnp.where(rows == i, m_ref[(k * ROWS + i) * slots + m], column)
            columns.append(column)
    column = jnp.concatenate(columns, axis=0)
    value = column.astype(f32)
    weight = jnp.where(column == 0, 1.0, 2.0).astype(f32)
    lanes = lane_index(column.shape)

    me = lax.axis_index("grp")
    width = LANES // ROWS
    phases = phase_ref[pl.ds(me // ROWS, 1), :]
    spot = lane_index(phases.shape)
    moved = pltpu.roll(phases, (ROWS - me % ROWS) % ROWS * width, 1)
    local = jnp.where(spot < width, moved, 0.0)
    for k in (1, 2, 4):
        local = local + pltpu.roll(local, k * width, 1)
    turn = value * local
    cosine = jnp.cos(turn)
    sine = jnp.sin(turn)
    cos_ref[...] = cosine
    sin_ref[...] = jnp.where(lanes < LANES // 2, -sine, sine)

    def wrap(index):
        return index & (total - 1) if total & (total - 1) == 0 else index % total

    step = full_turn / total
    start = lax.axis_index("sec") * count
    fine = wrap(column * lanes).astype(f32) * step
    coarse = wrap(column * (start + lanes * LANES)).astype(f32) * step
    fine_cos, fine_sin = jnp.cos(fine), jnp.sin(fine)
    coarse_cos, coarse_sin = weight * jnp.cos(coarse), weight * jnp.sin(coarse)
    for a in range(count // LANES):
        cos_a = coarse_cos[:, a : a + 1]
        sin_a = coarse_sin[:, a : a + 1]
        block = jnp.concatenate([cos_a * fine_cos - sin_a * fine_sin, -(sin_a * fine_cos + cos_a * fine_sin)], axis=0)
        high = block.astype(bf16)
        low = (block - high.astype(f32)).astype(bf16)
        here = slice(a * LANES, (a + 1) * LANES)
        table_ref[: 2 * total_m, here] = high
        table_ref[2 * total_m : 4 * total_m, here] = low
        table_ref[4 * total_m :, here] = high


def start_kernel(
    sections,
    cycles,
    m_hbm,
    phase_hbm,
    residual_hbm,
    direction_hbm,
    legendre_hbm,
    send_ref,
    table_ref,
    cos_ref,
    sin_ref,
    legendre_ref,
    r_ref,
    d_ref,
    m_ref,
    phase_ref,
    residual_ref,
    direction_ref,
    small_sems,
    value_sems,
    legendre_sems,
):
    slots = r_ref.shape[0]
    small = [
        pltpu.make_async_copy(m_hbm, m_ref, small_sems.at[0]),
        pltpu.make_async_copy(phase_hbm, phase_ref, small_sems.at[1]),
    ]
    for copy in small:
        copy.start()
    copies = [
        pltpu.make_async_copy(direction_hbm, direction_ref, value_sems.at[0]),
        pltpu.make_async_copy(residual_hbm, residual_ref, value_sems.at[1]),
    ]
    blocks = [
        pltpu.make_async_copy(legendre_hbm.at[m], legendre_ref.at[m], legendre_sems.at[m]) for m in range(slots)
    ]
    copies[0].start()
    for block in blocks:
        block.start()
    copies[1].start()
    for copy in small:
        copy.wait()
    fill_tables(slots, table_ref.shape[1] * sections, m_ref, phase_ref, table_ref, cos_ref, sin_ref)
    copies[0].wait()
    for m in range(slots):
        d = jnp.concatenate([direction_ref[0, m], direction_ref[1, m]], axis=0)
        d_ref[m] = d
        blocks[m].wait()
        forward_send(d, legendre_ref, send_ref, m, sections, cycles)
    copies[1].wait()
    square = None
    for m in range(slots):
        r = jnp.concatenate([residual_ref[0, m], residual_ref[1, m]], axis=0)
        r_ref[m] = r
        square = r * r if square is None else square + r * r
    send_scalars(send_ref, row_totals(square), slots)


def pixel_kernel(
    sections,
    chunk,
    first,
    last,
    recv_ref,
    table_ref,
    cos_ref,
    sin_ref,
    qq_ref,
    qu_ref,
    uu_ref,
    mask_ref,
    prior_ref,
    d_ref,
    *refs,
):
    if not first:
        r_ref, field_ref, rr_ref, *refs = refs
    send_ref, rr_out, *refs = refs
    if not first:
        d_out, *refs = refs
    if not last:
        (field_out,) = refs
    total_m = cos_ref.shape[0]
    slots = d_ref.shape[0]
    groups = total_m // slots
    tiles = [received_tile(recv_ref, m, k, sections) for m in range(slots) for k in range(groups // ROWS)]
    field = jnp.concatenate(tiles, axis=0)
    scalars = received_scalars(recv_ref, slots)
    rr_out[...] = scalars
    if not first:
        now, before = pair(scalars), pair(rr_ref[...])
        ratio = tuple(a / b for a, b in zip(now, before))
        field = field + by_lane(ratio, field.shape) * field_ref[...]
    if not last:
        field_out[...] = field
    half = LANES // 2
    cosine, sine = cos_ref[...], sin_ref[...]
    turned = field * cosine + pltpu.roll(field, half, 1) * sine
    modes = jnp.concatenate([turned[:, :half], turned[:, half:]], axis=0)
    high = modes.astype(bf16).astype(f32)
    rows3 = jnp.concatenate([high, high, modes - high], axis=0).astype(bf16)
    count = qq_ref.shape[1]
    cycles = qq_ref.shape[0]
    back = None
    curve = [None, None]
    for c in range(count // chunk):
        here = slice(c * chunk, (c + 1) * chunk)
        pixels = lax.dot_general(
            rows3, table_ref[:, here], (((0,), (0,)), ((), ())), preferred_element_type=f32
        )
        mask = mask_ref[:, here].astype(f32)
        nqq, nqu, nuu = mask * qq_ref[:, here], mask * qu_ref[:, here], mask * uu_ref[:, here]
        parts = []
        for b in range(2):
            q = pixels[2 * b * cycles : (2 * b + 1) * cycles]
            u = pixels[(2 * b + 1) * cycles : (2 * b + 2) * cycles]
            wq = nqq * q + nqu * u
            wu = nqu * q + nuu * u
            parts += [wq, wu]
            product = wq * q + wu * u
            curve[b] = product if curve[b] is None else curve[b] + product
        weighted = jnp.concatenate(parts, axis=0)
        high = weighted.astype(bf16).astype(f32)
        both = jnp.concatenate([high, weighted - high], axis=0).astype(bf16)
        part = lax.dot_general(
            table_ref[: 4 * total_m, here], both, (((1,), (1,)), ((), ())), preferred_element_type=f32
        )
        back = part if back is None else back + part
    top = 2 * total_m
    folded = back[:top, :half] + (back[:top, half:] + back[top:, :half])
    folded = jnp.concatenate([folded[:total_m], folded[total_m:]], axis=1)
    out = folded * cosine - pltpu.roll(folded, half, 1) * sine
    for m in range(slots):
        for k in range(groups // ROWS):
            at = (m * (groups // ROWS) + k) * ROWS
            for s in range(sections):
                start = s * groups + k * ROWS
                send_ref[start : start + ROWS, 0, m * LANES : (m + 1) * LANES] = out[at : at + ROWS]

    prior = prior_rows(prior_ref)
    own = None
    for m in range(slots):
        d = d_ref[m]
        if not first:
            d = r_ref[m] + by_row(ratio, (ROWS, LANES))[:, :1] * d
            d_out[m] = d
        product = prior * d * d
        own = product if own is None else own + product

    def fold(x):
        x = jnp.sum(x, axis=0, keepdims=True)
        tile = x[:, :LANES]
        for k in range(1, x.shape[1] // LANES):
            tile = tile + x[:, k * LANES : (k + 1) * LANES]
        return tile

    send_scalars(send_ref, join_halves(fold(curve[0]), fold(curve[1])) + row_totals(own), slots)


def prior_rows(prior_ref):
    e = prior_ref[0:1, :]
    b = prior_ref[1:2, :]
    shape = (ROWS, prior_ref.shape[1])
    return jnp.where((row_index(shape) >> 1) & 1 == 0, jnp.broadcast_to(e, shape), jnp.broadcast_to(b, shape))


def image_step(sections, cycles, recv_ref, rr_ref, prior_ref, legendre_ref, r_ref, d_ref, m, alpha, prior):
    tiles = []
    for k in range(cycles // LANES):
        tiles.append(permute_rows(swap_blocks(received_tile(recv_ref, m, k, sections)), from_message))
    field = jnp.concatenate(tiles, axis=1) if len(tiles) > 1 else tiles[0]
    both = split_rows(jnp.concatenate([-field, flip_signed(field)], axis=1))
    image = jnp.dot(both, legendre_ref[m], preferred_element_type=f32)
    image = (image[:ROWS] + image[ROWS:]) + prior * d_ref[m]
    return r_ref[m] - alpha * image


def step_size(recv_ref, rr_ref, slots):
    curve = pair(received_scalars(recv_ref, slots))
    two = tuple(a / b for a, b in zip(pair(rr_ref[...]), curve))
    return by_row(two, (ROWS, LANES))[:, :1]


def update_kernel(
    sections, cycles, first, recv_ref, rr_ref, prior_ref, legendre_ref, r_ref, d_ref, *refs
):
    if not first:
        x_ref, *refs = refs
    send_ref, r_out, x_out = refs
    slots = r_ref.shape[0]
    alpha = step_size(recv_ref, rr_ref, slots)
    prior = prior_rows(prior_ref)
    square = None
    for m in range(slots):
        r = image_step(sections, cycles, recv_ref, rr_ref, prior_ref, legendre_ref, r_ref, d_ref, m, alpha, prior)
        r_out[m] = r
        square = r * r if square is None else square + r * r
        forward_send(r, legendre_ref, send_ref, m, sections, cycles)
        x_out[m] = alpha * d_ref[m] if first else x_ref[m] + alpha * d_ref[m]
    send_scalars(send_ref, row_totals(square), slots)


def last_kernel(
    sections,
    cycles,
    recv_ref,
    rr_ref,
    prior_ref,
    legendre_ref,
    r_ref,
    d_ref,
    x_ref,
    solution_ref,
    send_ref,
    residual_out,
    solution_out,
    r_out,
):
    slots = r_ref.shape[0]
    alpha = step_size(recv_ref, rr_ref, slots)
    prior = prior_rows(prior_ref)
    square = None
    for m in range(slots):
        r = image_step(sections, cycles, recv_ref, rr_ref, prior_ref, legendre_ref, r_ref, d_ref, m, alpha, prior)
        square = r * r if square is None else square + r * r
        x = x_ref[m] + alpha * d_ref[m]
        r_out[m] = r
        for b in range(2):
            residual_out[b, m] = r[4 * b : 4 * b + 4]
            solution_out[b, m] = solution_ref[b, m] + x[4 * b : 4 * b + 4]
    send_scalars(send_ref, row_totals(square), 0)


def end_kernel(recv_ref, rr_ref, d_ref, r_ref, direction_out):
    slots = d_ref.shape[0]
    now, before = pair(received_scalars(recv_ref, 0)), pair(rr_ref[...])
    for b in range(2):
        ratio = now[b] / before[b]
        for m in range(slots):
            here = slice(4 * b, 4 * b + 4)
            direction_out[b, m] = r_ref[m, here] + ratio * d_ref[m, here]


def call(kernel, outs, name, limit=24 << 20, hbm=(), scratch=()):
    def run(*args):
        vmem = pl.BlockSpec(memory_space=pltpu.VMEM)
        specs = [vmem] * len(args)
        args = list(args)
        for i in hbm:
            specs[i] = pl.BlockSpec(memory_space=pltpu.HBM)
            args[i] = pltpu.with_memory_space_constraint(args[i], pltpu.HBM)
        return pl.pallas_call(
            kernel,
            out_shape=[jax.ShapeDtypeStruct(shape, dtype) for shape, dtype in outs],
            in_specs=specs,
            out_specs=[vmem] * len(outs),
            scratch_shapes=list(scratch),
            compiler_params=pltpu.CompilerParams(vmem_limit_bytes=limit),
            name=name,
        )(*args)

    return run


def per_device(
    solution_in,
    residual_in,
    direction_in,
    legendre,
    inverse_prior,
    noise_qq,
    noise_qu,
    noise_uu,
    pixel_mask,
    cycle_phase,
    m_values,
):
    sections = lax.axis_size("sec")
    devices = sections * lax.axis_size("grp")
    slots, cycles, length = legendre.shape[0], legendre.shape[2], legendre.shape[3]
    total_m = m_values.shape[0]
    count = noise_qq.shape[1]
    message = ((devices, 1, (slots + 1) * LANES), f32)
    scalars = ((devices, 1, LANES), f32)
    inner = ((slots, ROWS, length), f32)
    outer = (solution_in.shape, f32)
    vector = ((1, LANES), f32)
    field_like = ((total_m, LANES), f32)
    chunk = min(512, count)

    def exchange(x):
        return lax.all_to_all(x, ("sec", "grp"), 0, 0, tiled=True)

    table = ((6 * total_m, count), bf16)
    blocks = ((slots, 2 * cycles, length), bf16)
    send, trig, cosine, sine, rows, r, d = call(
        functools.partial(start_kernel, sections, cycles),
        [message, table, field_like, field_like, blocks, inner, inner],
        "start",
        hbm=range(5),
        scratch=(
            pltpu.SMEM((total_m,), jnp.int32),
            pltpu.VMEM((cycle_phase.shape[0] // LANES, LANES), f32),
            pltpu.VMEM(residual_in.shape, f32),
            pltpu.VMEM(direction_in.shape, f32),
            pltpu.SemaphoreType.DMA((2,)),
            pltpu.SemaphoreType.DMA((2,)),
            pltpu.SemaphoreType.DMA((slots,)),
        ),
    )(m_values, cycle_phase.reshape(-1, LANES), residual_in, direction_in, legendre.reshape(blocks[0]))
    noise = (noise_qq, noise_qu, noise_uu, pixel_mask)
    for step in range(ITERS):
        first, last = step == 0, step == ITERS - 1
        recv = exchange(send)
        carried = () if first else (r, field, rr)
        out = call(
            functools.partial(pixel_kernel, sections, chunk, first, last),
            [message, vector] + ([] if first else [inner]) + ([] if last else [field_like]),
            "pixels",
        )(recv, trig, cosine, sine, *noise, inverse_prior, d, *carried)
        send, rr, *out = out
        if not first:
            d, *out = out
        if not last:
            (field,) = out
        recv = exchange(send)
        carried = (recv, rr, inverse_prior, rows, r, d) + (() if first else (x,))
        if last:
            send, residual, solution, r = call(
                functools.partial(last_kernel, sections, cycles), [scalars, outer, outer, inner], "last"
            )(*carried, solution_in)
        else:
            send, r, x = call(
                functools.partial(update_kernel, sections, cycles, first), [message, inner, inner], "update"
            )(*carried)
    recv = exchange(send)
    (direction,) = call(end_kernel, [outer], "end")(recv, rr, d, r)
    return solution, residual, direction


def solution(mesh):
    return jax.shard_map(
        per_device,
        mesh=mesh,
        in_specs=(
            P(None, "grp", None, "sec"),
            P(None, "grp", None, "sec"),
            P(None, "grp", None, "sec"),
            P("grp", None, None, "sec"),
            P(None, "sec"),
            P("grp", "sec"),
            P("grp", "sec"),
            P("grp", "sec"),
            P("grp", "sec"),
            P(),
            P(),
        ),
        out_specs=(
            P(None, "grp", None, "sec"),
            P(None, "grp", None, "sec"),
            P(None, "grp", None, "sec"),
        ),
        check_vma=False,
    )
```

```python
import functools
import math

import jax
import jax.numpy as jnp
from jax import lax
from jax.experimental import pallas as pl
from jax.experimental.pallas import tpu as pltpu
from jax.sharding import PartitionSpec as P

ITERS = 4
LANES = 128
ROWS = 8
full_turn = 2.0 * math.pi
f32 = jnp.float32
bf16 = jnp.bfloat16

to_message = tuple(b * 4 + p * 2 + q for q in (0, 1) for b in (0, 1) for p in (0, 1))
from_message = tuple(to_message.index(n) for n in range(ROWS))
flipped = tuple(n ^ 3 for n in range(ROWS))


def row_index(shape):
    return lax.broadcasted_iota(jnp.int32, shape, 0)


def lane_index(shape):
    return lax.broadcasted_iota(jnp.int32, shape, 1)


def permute_rows(x, order):
    rows = row_index(x.shape)
    by_shift = {}
    for t, n in enumerate(order):
        by_shift.setdefault((t - n) % ROWS, []).append(t)
    out = None
    for shift, targets in by_shift.items():
        moved = pltpu.roll(x, shift, 0) if shift else x
        if out is None:
            out = moved
        else:
            mask = functools.reduce(jnp.logical_or, [rows == t for t in targets])
            out = jnp.where(mask, moved, out)
    return out


def swap_blocks(x):
    width = LANES // ROWS
    rows = row_index(x.shape)
    block = lane_index(x.shape) // width
    for k in (4, 2, 1):
        row_bit = (rows & k) != 0
        block_bit = (block & k) != 0
        down = pltpu.roll(pltpu.roll(x, k, 0), (LANES - k * width) % LANES, 1)
        if k == 4:
            x = jnp.where(row_bit != block_bit, down, x)
        else:
            up = pltpu.roll(pltpu.roll(x, ROWS - k, 0), k * width, 1)
            x = jnp.where(row_bit == block_bit, x, jnp.where(row_bit, down, up))
    return x


def split_rows(x):
    high = x.astype(bf16).astype(f32)
    return jnp.concatenate([high, x - high], axis=0).astype(bf16)


def flip_signed(x):
    rows = row_index(x.shape)
    same = ((rows >> 1) & 1) == (rows & 1)
    moved = permute_rows(x, flipped)
    return jnp.where(same, moved, -moved)


def row_totals(x):
    tile = x[:, :LANES]
    for k in range(1, x.shape[1] // LANES):
        tile = tile + x[:, k * LANES : (k + 1) * LANES]
    rows = row_index(tile.shape)
    first = jnp.sum(jnp.where(rows < 4, tile, 0.0), axis=0, keepdims=True)
    second = jnp.sum(jnp.where(rows < 4, 0.0, tile), axis=0, keepdims=True)
    return join_halves(first, second)


def join_halves(first, second):
    first = first + pltpu.roll(first, LANES // 2, 1)
    second = second + pltpu.roll(second, LANES // 2, 1)
    return jnp.where(lane_index(first.shape) < LANES // 2, first, second)


def pair(vector):
    low = lane_index(vector.shape) < LANES // 2
    return (
        jnp.sum(jnp.where(low, vector, 0.0), axis=1, keepdims=True),
        jnp.sum(jnp.where(low, 0.0, vector), axis=1, keepdims=True),
    )


def by_row(two, shape):
    return jnp.where(row_index(shape) < 4, two[0], two[1])


def by_lane(two, shape):
    quarter = LANES // 4
    return jnp.where((lane_index(shape) // quarter) % 2 == 0, two[0], two[1])


def forward_product(values, legendre_ref, m):
    return lax.dot_general(
        split_rows(values),
        legendre_ref[m],
        (((1,), (1,)), ((), ())),
        preferred_element_type=f32,
    )


def forward_send(prod, send_ref, m, sections, cycles, slots):
    prod = prod[:ROWS] + prod[ROWS:]
    field = flip_signed(prod[:, cycles:]) - prod[:, :cycles]
    field = permute_rows(field, to_message)
    for k in range(cycles // LANES):
        send_tile(send_ref, swap_blocks(field[:, k * LANES : (k + 1) * LANES]), m, k, sections, slots)


def tile_rows(ref, m, k, s, sections, slots):
    groups = ref.shape[0] // (slots + 1) // sections
    return pl.ds((s * groups + k * ROWS) * (slots + 1) + m, ROWS, stride=slots + 1)


def send_tile(send_ref, tile, m, k, sections, slots):
    for s in range(sections):
        send_ref[tile_rows(send_ref, m, k, s, sections, slots), :] = tile


def scalar_rows(ref, slots):
    count = ref.shape[0] // (slots + 1)
    return pl.ds(slots, count, stride=slots + 1) if slots else slice(None)


def send_scalars(send_ref, vector, slots):
    count = send_ref.shape[0] // (slots + 1)
    send_ref[scalar_rows(send_ref, slots), :] = jnp.broadcast_to(vector, (count, LANES))


def received_scalars(recv_ref, slots):
    return jnp.sum(recv_ref[scalar_rows(recv_ref, slots), :], axis=0, keepdims=True)


def received_tile(recv_ref, m, k, sections, slots):
    total = None
    for s in range(sections):
        part = recv_ref[tile_rows(recv_ref, m, k, s, sections, slots), :]
        total = part if total is None else total + part
    return total


def fill_tables(slots, total, m_ref, phase_ref, table_ref, cos_ref, sin_ref):
    total_m = cos_ref.shape[0]
    count = table_ref.shape[1]
    groups = total_m // slots
    rows = row_index((ROWS, LANES))
    columns = []
    for m in range(slots):
        for k in range(groups // ROWS):
            column = jnp.zeros((ROWS, LANES), jnp.int32)
            for i in range(ROWS):
                column = jnp.where(rows == i, m_ref[(k * ROWS + i) * slots + m], column)
            columns.append(column)
    column = jnp.concatenate(columns, axis=0)
    value = column.astype(f32)
    weight = jnp.where(column == 0, 1.0, 2.0).astype(f32)
    lanes = lane_index(column.shape)

    me = lax.axis_index("grp")
    width = LANES // ROWS
    phases = phase_ref[pl.ds(me // ROWS, 1), :]
    spot = lane_index(phases.shape)
    moved = pltpu.roll(phases, (ROWS - me % ROWS) % ROWS * width, 1)
    local = jnp.where(spot < width, moved, 0.0)
    for k in (1, 2, 4):
        local = local + pltpu.roll(local, k * width, 1)
    turn = value * local
    cosine = jnp.cos(turn)
    sine = jnp.sin(turn)
    cos_ref[...] = cosine
    sin_ref[...] = jnp.where(lanes < LANES // 2, -sine, sine)

    def wrap(index):
        return index & (total - 1) if total & (total - 1) == 0 else index % total

    step = full_turn / total
    start = lax.axis_index("sec") * count
    fine = wrap(column * lanes).astype(f32) * step
    coarse = wrap(column * (start + lanes * LANES)).astype(f32) * step
    fine_cos, fine_sin = jnp.cos(fine), jnp.sin(fine)
    coarse_cos, coarse_sin = weight * jnp.cos(coarse), weight * jnp.sin(coarse)
    for a in range(count // LANES):
        cos_a = coarse_cos[:, a : a + 1]
        sin_a = coarse_sin[:, a : a + 1]
        block = jnp.concatenate([cos_a * fine_cos - sin_a * fine_sin, -(sin_a * fine_cos + cos_a * fine_sin)], axis=0)
        block = block.astype(bf16)
        here = slice(a * LANES, (a + 1) * LANES)
        table_ref[: 2 * total_m, here] = block
        table_ref[2 * total_m :, here] = block


def start_kernel(
    sections,
    cycles,
    m_hbm,
    phase_hbm,
    residual_hbm,
    direction_hbm,
    legendre_hbm,
    send_ref,
    table_ref,
    cos_ref,
    sin_ref,
    legendre_ref,
    r_ref,
    d_ref,
    m_ref,
    phase_ref,
    residual_ref,
    direction_ref,
    small_sems,
    value_sems,
    legendre_sems,
):
    slots = r_ref.shape[0]
    small = [
        pltpu.make_async_copy(m_hbm, m_ref, small_sems.at[0]),
        pltpu.make_async_copy(phase_hbm, phase_ref, small_sems.at[1]),
    ]
    for copy in small:
        copy.start()
    copies = [
        pltpu.make_async_copy(direction_hbm, direction_ref, value_sems.at[0]),
        pltpu.make_async_copy(residual_hbm, residual_ref, value_sems.at[1]),
    ]
    blocks = [
        pltpu.make_async_copy(legendre_hbm.at[m], legendre_ref.at[m], legendre_sems.at[m]) for m in range(slots)
    ]
    for copy in copies:
        copy.start()
    for block in blocks:
        block.start()
    for copy in small:
        copy.wait()
    fill_tables(slots, table_ref.shape[1] * sections, m_ref, phase_ref, table_ref, cos_ref, sin_ref)
    copies[0].wait()
    rows = []
    for m in range(slots):
        d = jnp.concatenate([direction_ref[0, m], direction_ref[1, m]], axis=0)
        d_ref[m] = d
        rows.append(d)
    copies[1].wait()
    square = None
    for m in range(slots):
        r = jnp.concatenate([residual_ref[0, m], residual_ref[1, m]], axis=0)
        r_ref[m] = r
        square = r * r if square is None else square + r * r
    send_scalars(send_ref, row_totals(square), slots)
    for block in blocks:
        block.wait()
    for m in range(slots):
        forward_send(forward_product(rows[m], legendre_ref, m), send_ref, m, sections, cycles, slots)


def pixel_kernel(
    sections,
    chunk,
    first,
    last,
    recv_ref,
    table_ref,
    cos_ref,
    sin_ref,
    qq_ref,
    qu_ref,
    uu_ref,
    mask_ref,
    prior_ref,
    d_ref,
    *refs,
):
    if not first:
        r_ref, field_ref, rr_ref, *refs = refs
    send_ref, rr_out, *refs = refs
    if not first:
        d_out, *refs = refs
    if not last:
        (field_out,) = refs
    total_m = cos_ref.shape[0]
    slots = d_ref.shape[0]
    groups = total_m // slots
    tiles = [received_tile(recv_ref, m, k, sections, slots) for m in range(slots) for k in range(groups // ROWS)]
    field = jnp.concatenate(tiles, axis=0)
    scalars = received_scalars(recv_ref, slots)
    rr_out[...] = scalars
    if not first:
        now, before = pair(scalars), pair(rr_ref[...])
        ratio = tuple(a / b for a, b in zip(now, before))
        field = field + by_lane(ratio, field.shape) * field_ref[...]
    if not last:
        field_out[...] = field
    half = LANES // 2
    cosine, sine = cos_ref[...], sin_ref[...]
    turned = field * cosine + pltpu.roll(field, half, 1) * sine
    modes = jnp.concatenate([turned[:, :half], turned[:, half:]], axis=0)
    high = modes.astype(bf16).astype(f32)
    both = jnp.concatenate([high, modes - high], axis=0).astype(bf16)
    count = qq_ref.shape[1]
    cycles = qq_ref.shape[0]
    top = 2 * total_m
    folded = None
    for c in range(count // chunk):
        here = slice(c * chunk, (c + 1) * chunk)
        pixels = lax.dot_general(
            both, table_ref[:, here], (((0,), (0,)), ((), ())), preferred_element_type=f32
        )
        mask = mask_ref[:, here].astype(f32)
        nqq, nqu, nuu = mask * qq_ref[:, here], mask * qu_ref[:, here], mask * uu_ref[:, here]
        parts = []
        for b in range(2):
            q = pixels[2 * b * cycles : (2 * b + 1) * cycles]
            u = pixels[(2 * b + 1) * cycles : (2 * b + 2) * cycles]
            parts += [nqq * q + nqu * u, nqu * q + nuu * u]
        weighted = jnp.concatenate(parts, axis=0).astype(bf16)
        part = lax.dot_general(
            table_ref[:top, here], weighted, (((1,), (1,)), ((), ())), preferred_element_type=f32
        )
        folded = part if folded is None else folded + part
    folded = jnp.concatenate([folded[:total_m], folded[total_m:]], axis=1)
    out = folded * cosine - pltpu.roll(folded, half, 1) * sine
    curve = jnp.sum(field * out, axis=0, keepdims=True)
    first_side = (lane_index(curve.shape) // (half // 2)) % 2 == 0
    curve = join_halves(jnp.where(first_side, curve, 0.0), jnp.where(first_side, 0.0, curve))
    for m in range(slots):
        for k in range(groups // ROWS):
            at = (m * (groups // ROWS) + k) * ROWS
            send_tile(send_ref, out[at : at + ROWS], m, k, sections, slots)

    prior = prior_rows(prior_ref)
    own = None
    for m in range(slots):
        d = d_ref[m]
        if not first:
            d = r_ref[m] + by_row(ratio, (ROWS, LANES))[:, :1] * d
            d_out[m] = d
        product = prior * d * d
        own = product if own is None else own + product

    send_scalars(send_ref, curve + row_totals(own), slots)


def prior_rows(prior_ref):
    e = prior_ref[0:1, :]
    b = prior_ref[1:2, :]
    shape = (ROWS, prior_ref.shape[1])
    return jnp.where((row_index(shape) >> 1) & 1 == 0, jnp.broadcast_to(e, shape), jnp.broadcast_to(b, shape))


def image_terms(recv_ref, m, sections, cycles, slots):
    tiles = []
    for k in range(cycles // LANES):
        tiles.append(permute_rows(swap_blocks(received_tile(recv_ref, m, k, sections, slots)), from_message))
    field = jnp.concatenate(tiles, axis=1) if len(tiles) > 1 else tiles[0]
    return split_rows(jnp.concatenate([-field, flip_signed(field)], axis=1))


def next_residual(both, legendre_ref, r_ref, d_ref, m, alpha, prior):
    image = jnp.dot(both, legendre_ref[m], preferred_element_type=f32)
    image = (image[:ROWS] + image[ROWS:]) + prior * d_ref[m]
    return r_ref[m] - alpha * image


def step_size(recv_ref, rr_ref, slots):
    curve = pair(received_scalars(recv_ref, slots))
    two = tuple(a / b for a, b in zip(pair(rr_ref[...]), curve))
    return by_row(two, (ROWS, LANES))[:, :1]


def update_kernel(
    sections, cycles, first, recv_ref, rr_ref, prior_ref, legendre_ref, r_ref, d_ref, *refs
):
    if not first:
        x_ref, *refs = refs
    send_ref, r_out, x_out = refs
    slots = r_ref.shape[0]
    alpha = step_size(recv_ref, rr_ref, slots)
    prior = prior_rows(prior_ref)
    square = None
    terms = [image_terms(recv_ref, m, sections, cycles, slots) for m in range(slots)]
    for m in range(slots):
        r = next_residual(terms[m], legendre_ref, r_ref, d_ref, m, alpha, prior)
        r_out[m] = r
        square = r * r if square is None else square + r * r
        forward_send(forward_product(r, legendre_ref, m), send_ref, m, sections, cycles, slots)
        x_out[m] = alpha * d_ref[m] if first else x_ref[m] + alpha * d_ref[m]
    send_scalars(send_ref, row_totals(square), slots)


def last_kernel(
    sections,
    cycles,
    recv_ref,
    rr_ref,
    prior_ref,
    legendre_ref,
    r_ref,
    d_ref,
    x_ref,
    solution_ref,
    send_ref,
    residual_out,
    solution_out,
    r_out,
):
    slots = r_ref.shape[0]
    alpha = step_size(recv_ref, rr_ref, slots)
    prior = prior_rows(prior_ref)
    square = None
    terms = [image_terms(recv_ref, m, sections, cycles, slots) for m in range(slots)]
    for m in range(slots):
        r = next_residual(terms[m], legendre_ref, r_ref, d_ref, m, alpha, prior)
        square = r * r if square is None else square + r * r
        x = x_ref[m] + alpha * d_ref[m]
        r_out[m] = r
        for b in range(2):
            residual_out[b, m] = r[4 * b : 4 * b + 4]
            solution_out[b, m] = solution_ref[b, m] + x[4 * b : 4 * b + 4]
    send_scalars(send_ref, row_totals(square), 0)


def end_kernel(recv_ref, rr_ref, d_ref, r_ref, direction_out):
    slots = d_ref.shape[0]
    now, before = pair(received_scalars(recv_ref, 0)), pair(rr_ref[...])
    for b in range(2):
        ratio = now[b] / before[b]
        for m in range(slots):
            here = slice(4 * b, 4 * b + 4)
            direction_out[b, m] = r_ref[m, here] + ratio * d_ref[m, here]


def call(kernel, outs, name, limit=24 << 20, hbm=(), scratch=()):
    def run(*args):
        vmem = pl.BlockSpec(memory_space=pltpu.VMEM)
        specs = [vmem] * len(args)
        args = list(args)
        for i in hbm:
            specs[i] = pl.BlockSpec(memory_space=pltpu.HBM)
            args[i] = pltpu.with_memory_space_constraint(args[i], pltpu.HBM)
        return pl.pallas_call(
            kernel,
            out_shape=[jax.ShapeDtypeStruct(shape, dtype) for shape, dtype in outs],
            in_specs=specs,
            out_specs=[vmem] * len(outs),
            scratch_shapes=list(scratch),
            compiler_params=pltpu.CompilerParams(vmem_limit_bytes=limit),
            name=name,
        )(*args)

    return run


def per_device(
    solution_in,
    residual_in,
    direction_in,
    legendre,
    inverse_prior,
    noise_qq,
    noise_qu,
    noise_uu,
    pixel_mask,
    cycle_phase,
    m_values,
):
    sections = lax.axis_size("sec")
    devices = sections * lax.axis_size("grp")
    slots, cycles, length = legendre.shape[0], legendre.shape[2], legendre.shape[3]
    total_m = m_values.shape[0]
    count = noise_qq.shape[1]
    message = ((devices * (slots + 1), LANES), f32)
    scalars = ((devices, LANES), f32)
    inner = ((slots, ROWS, length), f32)
    outer = (solution_in.shape, f32)
    vector = ((1, LANES), f32)
    field_like = ((total_m, LANES), f32)
    chunk = min(256, count)

    def exchange(x):
        blocks = x.reshape(devices, 1, x.size // devices)
        return lax.all_to_all(blocks, ("sec", "grp"), 0, 0, tiled=True).reshape(x.shape)

    table = ((4 * total_m, count), bf16)
    blocks = ((slots, 2 * cycles, length), bf16)
    send, trig, cosine, sine, rows, r, d = call(
        functools.partial(start_kernel, sections, cycles),
        [message, table, field_like, field_like, blocks, inner, inner],
        "start",
        hbm=range(5),
        scratch=(
            pltpu.SMEM((total_m,), jnp.int32),
            pltpu.VMEM((cycle_phase.shape[0] // LANES, LANES), f32),
            pltpu.VMEM(residual_in.shape, f32),
            pltpu.VMEM(direction_in.shape, f32),
            pltpu.SemaphoreType.DMA((2,)),
            pltpu.SemaphoreType.DMA((2,)),
            pltpu.SemaphoreType.DMA((slots,)),
        ),
    )(m_values, cycle_phase.reshape(-1, LANES), residual_in, direction_in, legendre.reshape(blocks[0]))
    noise = (noise_qq, noise_qu, noise_uu, pixel_mask)
    for step in range(ITERS):
        first, last = step == 0, step == ITERS - 1
        recv = exchange(send)
        carried = () if first else (r, field, rr)
        out = call(
            functools.partial(pixel_kernel, sections, chunk, first, last),
            [message, vector] + ([] if first else [inner]) + ([] if last else [field_like]),
            "pixels",
        )(recv, trig, cosine, sine, *noise, inverse_prior, d, *carried)
        send, rr, *out = out
        if not first:
            d, *out = out
        if not last:
            (field,) = out
        recv = exchange(send)
        carried = (recv, rr, inverse_prior, rows, r, d) + (() if first else (x,))
        if last:
            send, residual, solution, r = call(
                functools.partial(last_kernel, sections, cycles), [scalars, outer, outer, inner], "last"
            )(*carried, solution_in)
        else:
            send, r, x = call(
                functools.partial(update_kernel, sections, cycles, first), [message, inner, inner], "update"
            )(*carried)
    recv = exchange(send)
    (direction,) = call(end_kernel, [outer], "end")(recv, rr, d, r)
    return solution, residual, direction


def solution(mesh):
    return jax.shard_map(
        per_device,
        mesh=mesh,
        in_specs=(
            P(None, "grp", None, "sec"),
            P(None, "grp", None, "sec"),
            P(None, "grp", None, "sec"),
            P("grp", None, None, "sec"),
            P(None, "sec"),
            P("grp", "sec"),
            P("grp", "sec"),
            P("grp", "sec"),
            P("grp", "sec"),
            P(),
            P(),
        ),
        out_specs=(
            P(None, "grp", None, "sec"),
            P(None, "grp", None, "sec"),
            P(None, "grp", None, "sec"),
        ),
        check_vma=False,
    )
```

```python
import functools
import math

import jax
import jax.numpy as jnp
from jax import lax
from jax.experimental import pallas as pl
from jax.experimental.pallas import tpu as pltpu
from jax.sharding import PartitionSpec as P

ITERS = 4
LANES = 128
ROWS = 8
full_turn = 2.0 * math.pi
f32 = jnp.float32
bf16 = jnp.bfloat16

flipped = tuple(n ^ 3 for n in range(ROWS))


def row_index(shape):
    return lax.broadcasted_iota(jnp.int32, shape, 0)


def lane_index(shape):
    return lax.broadcasted_iota(jnp.int32, shape, 1)


def permute_rows(x, order):
    rows = row_index(x.shape)
    by_shift = {}
    for t, n in enumerate(order):
        by_shift.setdefault((t - n) % ROWS, []).append(t)
    out = None
    for shift, targets in by_shift.items():
        moved = pltpu.roll(x, shift, 0) if shift else x
        if out is None:
            out = moved
        else:
            mask = functools.reduce(jnp.logical_or, [rows == t for t in targets])
            out = jnp.where(mask, moved, out)
    return out


def turn_blocks(buffer_ref, start, stride, distance):
    width = LANES // ROWS
    out = None
    for k in range(ROWS):
        moved = buffer_ref[pl.ds(start + 4 * k, ROWS, stride=stride), :]
        out = moved if out is None else jnp.where(distance == k, pltpu.roll(moved, k * width, 1), out)
    return out


def store_copies(x, buffer_ref, starts, stride):
    for start in starts:
        buffer_ref[pl.ds(start, ROWS, stride=stride), :] = x


def to_rows(x, buffer_ref):
    store_copies(x, buffer_ref, (16, 48, 2, 34), 4)
    rows = row_index(x.shape)
    place = (rows & 1) * 4 + (rows >> 1)
    distance = (lane_index(x.shape) // (LANES // ROWS) - place) & (ROWS - 1)
    return turn_blocks(buffer_ref, 16, 2, distance)


def to_message(x, buffer_ref):
    store_copies(x, buffer_ref, (0, 14, 32, 46), 2)
    distance = (lane_index(x.shape) // (LANES // ROWS) - row_index(x.shape)) & (ROWS - 1)
    return turn_blocks(buffer_ref, 0, 4, distance)


def split_rows(x):
    high = x.astype(bf16).astype(f32)
    return jnp.concatenate([high, x - high], axis=0).astype(bf16)


def flip_signed(x):
    rows = row_index(x.shape)
    same = ((rows >> 1) & 1) == (rows & 1)
    moved = permute_rows(x, flipped)
    return jnp.where(same, moved, -moved)


def row_totals(x):
    tile = x[:, :LANES]
    for k in range(1, x.shape[1] // LANES):
        tile = tile + x[:, k * LANES : (k + 1) * LANES]
    rows = row_index(tile.shape)
    first = jnp.sum(jnp.where(rows < 4, tile, 0.0), axis=0, keepdims=True)
    second = jnp.sum(jnp.where(rows < 4, 0.0, tile), axis=0, keepdims=True)
    return join_halves(first, second)


def join_halves(first, second):
    first = first + pltpu.roll(first, LANES // 2, 1)
    second = second + pltpu.roll(second, LANES // 2, 1)
    return jnp.where(lane_index(first.shape) < LANES // 2, first, second)


def pair(vector):
    low = lane_index(vector.shape) < LANES // 2
    return (
        jnp.sum(jnp.where(low, vector, 0.0), axis=1, keepdims=True),
        jnp.sum(jnp.where(low, 0.0, vector), axis=1, keepdims=True),
    )


def by_row(two, shape):
    return jnp.where(row_index(shape) < 4, two[0], two[1])


def by_lane(two, shape):
    quarter = LANES // 4
    return jnp.where((lane_index(shape) // quarter) % 2 == 0, two[0], two[1])


def forward_product(values, legendre_ref, m):
    return lax.dot_general(
        split_rows(values),
        legendre_ref[m],
        (((1,), (1,)), ((), ())),
        preferred_element_type=f32,
    )


def forward_send(prod, send_ref, buffer_ref, m, sections, cycles, slots):
    prod = prod[:ROWS] + prod[ROWS:]
    field = flip_signed(prod[:, cycles:]) - prod[:, :cycles]
    for k in range(cycles // LANES):
        tile = field[:, k * LANES : (k + 1) * LANES]
        at = m * (cycles // LANES) + k
        send_tile(send_ref, to_message(tile, buffer_ref.at[at]), m, k, sections, slots)


def tile_rows(ref, m, k, s, sections, slots):
    groups = ref.shape[0] // (slots + 1) // sections
    return pl.ds((s * groups + k * ROWS) * (slots + 1) + m, ROWS, stride=slots + 1)


def send_tile(send_ref, tile, m, k, sections, slots):
    for s in range(sections):
        send_ref[tile_rows(send_ref, m, k, s, sections, slots), :] = tile


def scalar_rows(ref, slots):
    count = ref.shape[0] // (slots + 1)
    return pl.ds(slots, count, stride=slots + 1) if slots else slice(None)


def send_scalars(send_ref, vector, slots):
    count = send_ref.shape[0] // (slots + 1)
    send_ref[scalar_rows(send_ref, slots), :] = jnp.broadcast_to(vector, (count, LANES))


def received_scalars(recv_ref, slots):
    return jnp.sum(recv_ref[scalar_rows(recv_ref, slots), :], axis=0, keepdims=True)


def received_tile(recv_ref, m, k, sections, slots):
    total = None
    for s in range(sections):
        part = recv_ref[tile_rows(recv_ref, m, k, s, sections, slots), :]
        total = part if total is None else total + part
    return total


def fill_tables(slots, total, m_ref, phase_ref, table_ref, cos_ref, sin_ref):
    total_m = cos_ref.shape[0]
    count = table_ref.shape[1]
    groups = total_m // slots
    rows = row_index((ROWS, LANES))
    columns = []
    for m in range(slots):
        for k in range(groups // ROWS):
            column = jnp.zeros((ROWS, LANES), jnp.int32)
            for i in range(ROWS):
                column = jnp.where(rows == i, m_ref[(k * ROWS + i) * slots + m], column)
            columns.append(column)
    column = jnp.concatenate(columns, axis=0)
    value = column.astype(f32)
    weight = jnp.where(column == 0, 1.0, 2.0).astype(f32)
    lanes = lane_index(column.shape)

    me = lax.axis_index("grp")
    width = LANES // ROWS
    phases = phase_ref[pl.ds(me // ROWS, 1), :]
    spot = lane_index(phases.shape)
    moved = pltpu.roll(phases, (ROWS - me % ROWS) % ROWS * width, 1)
    local = jnp.where(spot < width, moved, 0.0)
    for k in (1, 2, 4):
        local = local + pltpu.roll(local, k * width, 1)
    turn = value * local
    cosine = jnp.cos(turn)
    sine = jnp.sin(turn)
    cos_ref[...] = cosine
    sin_ref[...] = jnp.where(lanes < LANES // 2, -sine, sine)

    def wrap(index):
        return index & (total - 1) if total & (total - 1) == 0 else index % total

    step = full_turn / total
    start = lax.axis_index("sec") * count
    fine = wrap(column * lanes).astype(f32) * step
    coarse = wrap(column * (start + lanes * LANES)).astype(f32) * step
    fine_cos, fine_sin = jnp.cos(fine), jnp.sin(fine)
    coarse_cos, coarse_sin = weight * jnp.cos(coarse), weight * jnp.sin(coarse)
    for a in range(count // LANES):
        cos_a = coarse_cos[:, a : a + 1]
        sin_a = coarse_sin[:, a : a + 1]
        block = jnp.concatenate([cos_a * fine_cos - sin_a * fine_sin, -(sin_a * fine_cos + cos_a * fine_sin)], axis=0)
        block = block.astype(bf16)
        here = slice(a * LANES, (a + 1) * LANES)
        table_ref[: 2 * total_m, here] = block
        table_ref[2 * total_m :, here] = block


def start_kernel(
    sections,
    cycles,
    m_hbm,
    phase_hbm,
    residual_hbm,
    direction_hbm,
    legendre_hbm,
    send_ref,
    table_ref,
    cos_ref,
    sin_ref,
    legendre_ref,
    r_ref,
    d_ref,
    m_ref,
    phase_ref,
    residual_ref,
    direction_ref,
    buffer_ref,
    small_sems,
    value_sems,
    legendre_sems,
):
    slots = r_ref.shape[0]
    small = [
        pltpu.make_async_copy(m_hbm, m_ref, small_sems.at[0]),
        pltpu.make_async_copy(phase_hbm, phase_ref, small_sems.at[1]),
    ]
    for copy in small:
        copy.start()
    copies = [
        pltpu.make_async_copy(direction_hbm, direction_ref, value_sems.at[0]),
        pltpu.make_async_copy(residual_hbm, residual_ref, value_sems.at[1]),
    ]
    blocks = [
        pltpu.make_async_copy(legendre_hbm.at[m], legendre_ref.at[m], legendre_sems.at[m]) for m in range(slots)
    ]
    for copy in copies:
        copy.start()
    for block in blocks:
        block.start()
    for copy in small:
        copy.wait()
    fill_tables(slots, table_ref.shape[1] * sections, m_ref, phase_ref, table_ref, cos_ref, sin_ref)
    copies[0].wait()
    rows = []
    for m in range(slots):
        d = jnp.concatenate([direction_ref[0, m], direction_ref[1, m]], axis=0)
        d_ref[m] = d
        rows.append(d)
    copies[1].wait()
    square = None
    for m in range(slots):
        r = jnp.concatenate([residual_ref[0, m], residual_ref[1, m]], axis=0)
        r_ref[m] = r
        square = r * r if square is None else square + r * r
    send_scalars(send_ref, row_totals(square), slots)
    for block in blocks:
        block.wait()
    for m in range(slots):
        forward_send(forward_product(rows[m], legendre_ref, m), send_ref, buffer_ref, m, sections, cycles, slots)


def pixel_kernel(
    sections,
    chunk,
    first,
    last,
    recv_ref,
    table_ref,
    cos_ref,
    sin_ref,
    qq_ref,
    qu_ref,
    uu_ref,
    mask_ref,
    prior_ref,
    d_ref,
    *refs,
):
    if not first:
        r_ref, field_ref, rr_ref, *refs = refs
    send_ref, rr_out, *refs = refs
    if not first:
        d_out, *refs = refs
    if not last:
        (field_out,) = refs
    total_m = cos_ref.shape[0]
    slots = d_ref.shape[0]
    groups = total_m // slots
    tiles = [received_tile(recv_ref, m, k, sections, slots) for m in range(slots) for k in range(groups // ROWS)]
    field = jnp.concatenate(tiles, axis=0)
    scalars = received_scalars(recv_ref, slots)
    rr_out[...] = scalars
    if not first:
        now, before = pair(scalars), pair(rr_ref[...])
        ratio = tuple(a / b for a, b in zip(now, before))
        field = field + by_lane(ratio, field.shape) * field_ref[...]
    if not last:
        field_out[...] = field
    half = LANES // 2
    cosine, sine = cos_ref[...], sin_ref[...]
    turned = field * cosine + pltpu.roll(field, half, 1) * sine
    modes = jnp.concatenate([turned[:, :half], turned[:, half:]], axis=0)
    high = modes.astype(bf16).astype(f32)
    both = jnp.concatenate([high, modes - high], axis=0).astype(bf16)
    count = qq_ref.shape[1]
    cycles = qq_ref.shape[0]
    top = 2 * total_m
    folded = None
    for c in range(count // chunk):
        here = slice(c * chunk, (c + 1) * chunk)
        pixels = lax.dot_general(
            both, table_ref[:, here], (((0,), (0,)), ((), ())), preferred_element_type=f32
        )
        mask = mask_ref[:, here].astype(f32)
        nqq, nqu, nuu = mask * qq_ref[:, here], mask * qu_ref[:, here], mask * uu_ref[:, here]
        parts = []
        for b in range(2):
            q = pixels[2 * b * cycles : (2 * b + 1) * cycles]
            u = pixels[(2 * b + 1) * cycles : (2 * b + 2) * cycles]
            parts += [nqq * q + nqu * u, nqu * q + nuu * u]
        weighted = jnp.concatenate(parts, axis=0).astype(bf16)
        part = lax.dot_general(
            table_ref[:top, here], weighted, (((1,), (1,)), ((), ())), preferred_element_type=f32
        )
        folded = part if folded is None else folded + part
    folded = jnp.concatenate([folded[:total_m], folded[total_m:]], axis=1)
    out = folded * cosine - pltpu.roll(folded, half, 1) * sine
    curve = jnp.sum(field * out, axis=0, keepdims=True)
    first_side = (lane_index(curve.shape) // (half // 2)) % 2 == 0
    curve = join_halves(jnp.where(first_side, curve, 0.0), jnp.where(first_side, 0.0, curve))
    for m in range(slots):
        for k in range(groups // ROWS):
            at = (m * (groups // ROWS) + k) * ROWS
            send_tile(send_ref, out[at : at + ROWS], m, k, sections, slots)

    prior = prior_rows(prior_ref)
    own = None
    for m in range(slots):
        d = d_ref[m]
        if not first:
            d = r_ref[m] + by_row(ratio, (ROWS, LANES))[:, :1] * d
            d_out[m] = d
        product = prior * d * d
        own = product if own is None else own + product

    send_scalars(send_ref, curve + row_totals(own), slots)


def prior_rows(prior_ref):
    e = prior_ref[0:1, :]
    b = prior_ref[1:2, :]
    shape = (ROWS, prior_ref.shape[1])
    return jnp.where((row_index(shape) >> 1) & 1 == 0, jnp.broadcast_to(e, shape), jnp.broadcast_to(b, shape))


def image_terms(recv_ref, buffer_ref, m, sections, cycles, slots):
    tiles = []
    for k in range(cycles // LANES):
        at = m * (cycles // LANES) + k
        tile = received_tile(recv_ref, m, k, sections, slots)
        tiles.append(to_rows(tile, buffer_ref.at[at]))
    field = jnp.concatenate(tiles, axis=1) if len(tiles) > 1 else tiles[0]
    return split_rows(jnp.concatenate([-field, flip_signed(field)], axis=1))


def next_residual(both, legendre_ref, r_ref, d_ref, m, alpha, prior):
    image = jnp.dot(both, legendre_ref[m], preferred_element_type=f32)
    image = (image[:ROWS] + image[ROWS:]) + prior * d_ref[m]
    return r_ref[m] - alpha * image


def step_size(recv_ref, rr_ref, slots):
    curve = pair(received_scalars(recv_ref, slots))
    two = tuple(a / b for a, b in zip(pair(rr_ref[...]), curve))
    return by_row(two, (ROWS, LANES))[:, :1]


def update_kernel(
    sections, cycles, first, recv_ref, rr_ref, prior_ref, legendre_ref, r_ref, d_ref, *refs
):
    if not first:
        x_ref, *refs = refs
    send_ref, r_out, x_out, buffer_ref = refs
    slots = r_ref.shape[0]
    alpha = step_size(recv_ref, rr_ref, slots)
    prior = prior_rows(prior_ref)
    square = None
    terms = [image_terms(recv_ref, buffer_ref, m, sections, cycles, slots) for m in range(slots)]
    for m in range(slots):
        r = next_residual(terms[m], legendre_ref, r_ref, d_ref, m, alpha, prior)
        r_out[m] = r
        square = r * r if square is None else square + r * r
        forward_send(forward_product(r, legendre_ref, m), send_ref, buffer_ref, m, sections, cycles, slots)
        x_out[m] = alpha * d_ref[m] if first else x_ref[m] + alpha * d_ref[m]
    send_scalars(send_ref, row_totals(square), slots)


def last_kernel(
    sections,
    cycles,
    recv_ref,
    rr_ref,
    prior_ref,
    legendre_ref,
    r_ref,
    d_ref,
    x_ref,
    solution_ref,
    send_ref,
    residual_out,
    solution_out,
    buffer_ref,
):
    slots = r_ref.shape[0]
    alpha = step_size(recv_ref, rr_ref, slots)
    prior = prior_rows(prior_ref)
    for m in range(slots):
        x = x_ref[m] + alpha * d_ref[m]
        for b in range(2):
            solution_out[b, m] = solution_ref[b, m] + x[4 * b : 4 * b + 4]
    square = None
    terms = [image_terms(recv_ref, buffer_ref, m, sections, cycles, slots) for m in range(slots)]
    for m in range(slots):
        r = next_residual(terms[m], legendre_ref, r_ref, d_ref, m, alpha, prior)
        square = r * r if square is None else square + r * r
        for b in range(2):
            residual_out[b, m] = r[4 * b : 4 * b + 4]
    send_scalars(send_ref, row_totals(square), 0)


def end_kernel(
    recv_ref, rr_ref, d_ref, residual_ref, solution_ref, direction_hbm, residual_hbm, solution_hbm, direction_ref, sems
):
    slots = d_ref.shape[0]
    copies = [
        pltpu.make_async_copy(residual_ref, residual_hbm, sems.at[0]),
        pltpu.make_async_copy(solution_ref, solution_hbm, sems.at[1]),
        pltpu.make_async_copy(direction_ref, direction_hbm, sems.at[2]),
    ]
    copies[0].start()
    copies[1].start()
    now, before = pair(received_scalars(recv_ref, 0)), pair(rr_ref[...])
    ratios = [now[b] / before[b] for b in range(2)]

    def fill(m, carry):
        for b in range(2):
            direction_ref[b, m] = residual_ref[b, m] + ratios[b] * d_ref[m, 4 * b : 4 * b + 4]
        return carry

    lax.fori_loop(0, slots, fill, 0)
    copies[2].start()
    for copy in copies:
        copy.wait()


def call(kernel, outs, name, limit=24 << 20, hbm=(), scratch=(), hbm_outs=()):
    def run(*args):
        vmem = pl.BlockSpec(memory_space=pltpu.VMEM)
        specs = [vmem] * len(args)
        args = list(args)
        for i in hbm:
            specs[i] = pl.BlockSpec(memory_space=pltpu.HBM)
            args[i] = pltpu.with_memory_space_constraint(args[i], pltpu.HBM)
        return pl.pallas_call(
            kernel,
            out_shape=[jax.ShapeDtypeStruct(shape, dtype) for shape, dtype in outs],
            in_specs=specs,
            out_specs=[pl.BlockSpec(memory_space=pltpu.HBM) if i in hbm_outs else vmem for i in range(len(outs))],
            scratch_shapes=list(scratch),
            compiler_params=pltpu.CompilerParams(vmem_limit_bytes=limit),
            name=name,
        )(*args)

    return run


def per_device(
    solution_in,
    residual_in,
    direction_in,
    legendre,
    inverse_prior,
    noise_qq,
    noise_qu,
    noise_uu,
    pixel_mask,
    cycle_phase,
    m_values,
):
    sections = lax.axis_size("sec")
    devices = sections * lax.axis_size("grp")
    slots, cycles, length = legendre.shape[0], legendre.shape[2], legendre.shape[3]
    total_m = m_values.shape[0]
    count = noise_qq.shape[1]
    message = ((devices * (slots + 1), LANES), f32)
    scalars = ((devices, LANES), f32)
    inner = ((slots, ROWS, length), f32)
    outer = (solution_in.shape, f32)
    vector = ((1, LANES), f32)
    field_like = ((total_m, LANES), f32)
    chunk = min(256, count)

    buffers = (pltpu.VMEM((slots * (cycles // LANES), 10 * ROWS, LANES), f32),)

    def exchange(x):
        blocks = x.reshape(devices, 1, x.size // devices)
        return lax.all_to_all(blocks, ("sec", "grp"), 0, 0, tiled=True).reshape(x.shape)

    table = ((4 * total_m, count), bf16)
    blocks = ((slots, 2 * cycles, length), bf16)
    send, trig, cosine, sine, rows, r, d = call(
        functools.partial(start_kernel, sections, cycles),
        [message, table, field_like, field_like, blocks, inner, inner],
        "start",
        hbm=range(5),
        scratch=(
            pltpu.SMEM((total_m,), jnp.int32),
            pltpu.VMEM((cycle_phase.shape[0] // LANES, LANES), f32),
            pltpu.VMEM(residual_in.shape, f32),
            pltpu.VMEM(direction_in.shape, f32),
            *buffers,
            pltpu.SemaphoreType.DMA((2,)),
            pltpu.SemaphoreType.DMA((2,)),
            pltpu.SemaphoreType.DMA((slots,)),
        ),
    )(m_values, cycle_phase.reshape(-1, LANES), residual_in, direction_in, legendre.reshape(blocks[0]))
    noise = (noise_qq, noise_qu, noise_uu, pixel_mask)
    for step in range(ITERS):
        first, last = step == 0, step == ITERS - 1
        recv = exchange(send)
        carried = () if first else (r, field, rr)
        out = call(
            functools.partial(pixel_kernel, sections, chunk, first, last),
            [message, vector] + ([] if first else [inner]) + ([] if last else [field_like]),
            "pixels",
        )(recv, trig, cosine, sine, *noise, inverse_prior, d, *carried)
        send, rr, *out = out
        if not first:
            d, *out = out
        if not last:
            (field,) = out
        recv = exchange(send)
        carried = (recv, rr, inverse_prior, rows, r, d) + (() if first else (x,))
        if last:
            send, residual, solution = call(
                functools.partial(last_kernel, sections, cycles),
                [scalars, outer, outer],
                "last",
                scratch=buffers,
            )(*carried, solution_in)
        else:
            send, r, x = call(
                functools.partial(update_kernel, sections, cycles, first), [message, inner, inner], "update", scratch=buffers
            )(*carried)
    recv = exchange(send)
    direction, residual, solution = call(
        end_kernel,
        [outer, outer, outer],
        "end",
        hbm_outs=(0, 1, 2),
        scratch=(pltpu.VMEM(outer[0], f32), pltpu.SemaphoreType.DMA((3,))),
    )(recv, rr, d, residual, solution)
    return solution, residual, direction


def solution(mesh):
    return jax.shard_map(
        per_device,
        mesh=mesh,
        in_specs=(
            P(None, "grp", None, "sec"),
            P(None, "grp", None, "sec"),
            P(None, "grp", None, "sec"),
            P("grp", None, None, "sec"),
            P(None, "sec"),
            P("grp", "sec"),
            P("grp", "sec"),
            P("grp", "sec"),
            P("grp", "sec"),
            P(),
            P(),
        ),
        out_specs=(
            P(None, "grp", None, "sec"),
            P(None, "grp", None, "sec"),
            P(None, "grp", None, "sec"),
        ),
        check_vma=False,
    )
```

```python
import functools
import math

import jax
import jax.numpy as jnp
from jax import lax
from jax.experimental import pallas as pl
from jax.experimental.pallas import tpu as pltpu
from jax.sharding import PartitionSpec as P

ITERS = 4
LANES = 128
ROWS = 8
full_turn = 2.0 * math.pi
f32 = jnp.float32
bf16 = jnp.bfloat16

flipped = tuple(n ^ 3 for n in range(ROWS))


def row_index(shape):
    return lax.broadcasted_iota(jnp.int32, shape, 0)


def lane_index(shape):
    return lax.broadcasted_iota(jnp.int32, shape, 1)


def permute_rows(x, order):
    rows = row_index(x.shape)
    by_shift = {}
    for t, n in enumerate(order):
        by_shift.setdefault((t - n) % ROWS, []).append(t)
    out = None
    for shift, targets in by_shift.items():
        moved = pltpu.roll(x, shift, 0) if shift else x
        if out is None:
            out = moved
        else:
            mask = functools.reduce(jnp.logical_or, [rows == t for t in targets])
            out = jnp.where(mask, moved, out)
    return out


def turn_blocks(buffer_ref, start, stride, distance):
    width = LANES // ROWS
    out = None
    for k in range(ROWS):
        moved = buffer_ref[pl.ds(start + 4 * k, ROWS, stride=stride), :]
        out = moved if out is None else jnp.where(distance == k, pltpu.roll(moved, k * width, 1), out)
    return out


def store_copies(x, buffer_ref, starts, stride):
    for start in starts:
        buffer_ref[pl.ds(start, ROWS, stride=stride), :] = x


def to_rows(x, buffer_ref):
    store_copies(x, buffer_ref, (16, 48, 2, 34), 4)
    rows = row_index(x.shape)
    place = (rows & 1) * 4 + (rows >> 1)
    distance = (lane_index(x.shape) // (LANES // ROWS) - place) & (ROWS - 1)
    return turn_blocks(buffer_ref, 16, 2, distance)


def to_message(x, buffer_ref):
    store_copies(x, buffer_ref, (0, 14, 32, 46), 2)
    distance = (lane_index(x.shape) // (LANES // ROWS) - row_index(x.shape)) & (ROWS - 1)
    return turn_blocks(buffer_ref, 0, 4, distance)


def split_rows(x):
    high = x.astype(bf16).astype(f32)
    return jnp.concatenate([high, x - high], axis=0).astype(bf16)


def flip_signed(x):
    rows = row_index(x.shape)
    same = ((rows >> 1) & 1) == (rows & 1)
    moved = permute_rows(x, flipped)
    return jnp.where(same, moved, -moved)


def row_totals(x):
    tile = x[:, :LANES]
    for k in range(1, x.shape[1] // LANES):
        tile = tile + x[:, k * LANES : (k + 1) * LANES]
    rows = row_index(tile.shape)
    first = jnp.sum(jnp.where(rows < 4, tile, 0.0), axis=0, keepdims=True)
    second = jnp.sum(jnp.where(rows < 4, 0.0, tile), axis=0, keepdims=True)
    return join_halves(first, second)


def join_halves(first, second):
    first = first + pltpu.roll(first, LANES // 2, 1)
    second = second + pltpu.roll(second, LANES // 2, 1)
    return jnp.where(lane_index(first.shape) < LANES // 2, first, second)


def pair(vector):
    low = lane_index(vector.shape) < LANES // 2
    return (
        jnp.sum(jnp.where(low, vector, 0.0), axis=1, keepdims=True),
        jnp.sum(jnp.where(low, 0.0, vector), axis=1, keepdims=True),
    )


def spread(two):
    return by_lane(two, (1, LANES))


def unspread(vector):
    spot = lane_index(vector.shape)
    return [jnp.sum(jnp.where(spot == b * (LANES // 4), vector, 0.0), axis=1, keepdims=True) for b in range(2)]


def by_row(two, shape):
    return jnp.where(row_index(shape) < 4, two[0], two[1])


def by_lane(two, shape):
    quarter = LANES // 4
    return jnp.where((lane_index(shape) // quarter) % 2 == 0, two[0], two[1])


def forward_product(values, legendre_ref, m):
    return lax.dot_general(
        split_rows(values),
        legendre_ref[m],
        (((1,), (1,)), ((), ())),
        preferred_element_type=f32,
    )


def turned_product(values, turned_ref, m):
    return jnp.dot(split_rows(values), turned_ref[m], preferred_element_type=f32)


def forward_send(prod, send_ref, buffer_ref, m, sections, cycles, slots):
    prod = prod[:ROWS] + prod[ROWS:]
    field = flip_signed(prod[:, cycles:]) - prod[:, :cycles]
    for k in range(cycles // LANES):
        tile = field[:, k * LANES : (k + 1) * LANES]
        at = m * (cycles // LANES) + k
        send_tile(send_ref, to_message(tile, buffer_ref.at[at]), m, k, sections, slots)


def tile_rows(ref, m, k, s, sections, slots):
    groups = ref.shape[0] // (slots + 1) // sections
    return pl.ds((s * groups + k * ROWS) * (slots + 1) + m, ROWS, stride=slots + 1)


def send_tile(send_ref, tile, m, k, sections, slots):
    for s in range(sections):
        send_ref[tile_rows(send_ref, m, k, s, sections, slots), :] = tile


def scalar_rows(ref, slots):
    count = ref.shape[0] // (slots + 1)
    return pl.ds(slots, count, stride=slots + 1) if slots else slice(None)


def send_scalars(send_ref, vector, slots):
    count = send_ref.shape[0] // (slots + 1)
    send_ref[scalar_rows(send_ref, slots), :] = jnp.broadcast_to(vector, (count, LANES))


def received_scalars(recv_ref, slots):
    return jnp.sum(recv_ref[scalar_rows(recv_ref, slots), :], axis=0, keepdims=True)


def received_tile(recv_ref, m, k, sections, slots):
    total = None
    for s in range(sections):
        part = recv_ref[tile_rows(recv_ref, m, k, s, sections, slots), :]
        total = part if total is None else total + part
    return total


def fill_tables(slots, total, m_ref, phase_ref, table_ref, cos_ref, sin_ref):
    total_m = cos_ref.shape[0]
    count = table_ref.shape[1]
    groups = total_m // slots
    rows = row_index((ROWS, LANES))
    columns = []
    for m in range(slots):
        for k in range(groups // ROWS):
            column = jnp.zeros((ROWS, LANES), jnp.int32)
            for i in range(ROWS):
                column = jnp.where(rows == i, m_ref[(k * ROWS + i) * slots + m], column)
            columns.append(column)
    column = jnp.concatenate(columns, axis=0)
    value = column.astype(f32)
    weight = jnp.where(column == 0, 1.0, 2.0).astype(f32)
    lanes = lane_index(column.shape)

    me = lax.axis_index("grp")
    width = LANES // ROWS
    phases = phase_ref[pl.ds(me // ROWS, 1), :]
    spot = lane_index(phases.shape)
    moved = pltpu.roll(phases, (ROWS - me % ROWS) % ROWS * width, 1)
    local = jnp.where(spot < width, moved, 0.0)
    for k in (1, 2, 4):
        local = local + pltpu.roll(local, k * width, 1)
    turn = value * local
    cosine = jnp.cos(turn)
    sine = jnp.sin(turn)
    cos_ref[...] = cosine
    sin_ref[...] = jnp.where(lanes < LANES // 2, -sine, sine)

    def wrap(index):
        return index & (total - 1) if total & (total - 1) == 0 else index % total

    step = full_turn / total
    start = lax.axis_index("sec") * count
    fine = wrap(column * lanes).astype(f32) * step
    coarse = wrap(column * (start + lanes * LANES)).astype(f32) * step
    fine_cos, fine_sin = jnp.cos(fine), jnp.sin(fine)
    coarse_cos, coarse_sin = weight * jnp.cos(coarse), weight * jnp.sin(coarse)
    for a in range(count // LANES):
        cos_a = coarse_cos[:, a : a + 1]
        sin_a = coarse_sin[:, a : a + 1]
        block = jnp.concatenate([cos_a * fine_cos - sin_a * fine_sin, -(sin_a * fine_cos + cos_a * fine_sin)], axis=0)
        block = block.astype(bf16)
        here = slice(a * LANES, (a + 1) * LANES)
        table_ref[: 2 * total_m, here] = block
        table_ref[2 * total_m :, here] = block


def start_kernel(
    sections,
    cycles,
    m_hbm,
    phase_hbm,
    residual_hbm,
    direction_hbm,
    legendre_hbm,
    send_ref,
    table_ref,
    cos_ref,
    sin_ref,
    legendre_ref,
    r_ref,
    d_ref,
    m_ref,
    phase_ref,
    residual_ref,
    direction_ref,
    buffer_ref,
    small_sems,
    value_sems,
    legendre_sems,
):
    slots = r_ref.shape[0]
    small = [
        pltpu.make_async_copy(m_hbm, m_ref, small_sems.at[0]),
        pltpu.make_async_copy(phase_hbm, phase_ref, small_sems.at[1]),
    ]
    for copy in small:
        copy.start()
    copies = [
        pltpu.make_async_copy(direction_hbm, direction_ref, value_sems.at[0]),
        pltpu.make_async_copy(residual_hbm, residual_ref, value_sems.at[1]),
    ]
    blocks = [
        pltpu.make_async_copy(legendre_hbm.at[m], legendre_ref.at[m], legendre_sems.at[m]) for m in range(slots)
    ]
    for copy in copies:
        copy.start()
    for block in blocks:
        block.start()
    for copy in small:
        copy.wait()
    fill_tables(slots, table_ref.shape[1] * sections, m_ref, phase_ref, table_ref, cos_ref, sin_ref)
    copies[0].wait()
    rows = []
    for m in range(slots):
        d = jnp.concatenate([direction_ref[0, m], direction_ref[1, m]], axis=0)
        d_ref[m] = d
        rows.append(d)
    copies[1].wait()
    square = None
    for m in range(slots):
        r = jnp.concatenate([residual_ref[0, m], residual_ref[1, m]], axis=0)
        r_ref[m] = r
        square = r * r if square is None else square + r * r
    send_scalars(send_ref, spread(pair(row_totals(square))), slots)
    for block in blocks:
        block.wait()
    for m in range(slots):
        forward_send(forward_product(rows[m], legendre_ref, m), send_ref, buffer_ref, m, sections, cycles, slots)


def pixel_kernel(
    sections,
    chunk,
    first,
    last,
    recv_ref,
    table_ref,
    cos_ref,
    sin_ref,
    qq_ref,
    qu_ref,
    uu_ref,
    mask_ref,
    prior_ref,
    d_ref,
    *refs,
):
    if first:
        legendre_ref, *refs = refs
    else:
        r_ref, field_ref, rr_ref, *refs = refs
    send_ref, rr_out, *refs = refs
    if first:
        turned_ref, *refs = refs
        for m in range(legendre_ref.shape[0]):
            turned_ref[m] = legendre_ref[m].T
    if not first:
        d_out, *refs = refs
    if not last:
        (field_out,) = refs
    total_m = cos_ref.shape[0]
    slots = d_ref.shape[0]
    groups = total_m // slots
    tiles = [received_tile(recv_ref, m, k, sections, slots) for m in range(slots) for k in range(groups // ROWS)]
    field = jnp.concatenate(tiles, axis=0)
    scalars = received_scalars(recv_ref, slots)
    rr_out[...] = scalars
    if not first:
        lane_ratio = scalars / rr_ref[...]
        ratio = unspread(lane_ratio)
        field = field + lane_ratio * field_ref[...]
    if not last:
        field_out[...] = field
    half = LANES // 2
    cosine, sine = cos_ref[...], sin_ref[...]
    turned = field * cosine + pltpu.roll(field, half, 1) * sine
    modes = jnp.concatenate([turned[:, :half], turned[:, half:]], axis=0)
    high = modes.astype(bf16).astype(f32)
    both = jnp.concatenate([high, modes - high], axis=0).astype(bf16)
    count = qq_ref.shape[1]
    cycles = qq_ref.shape[0]
    top = 2 * total_m
    folded = None
    for c in range(count // chunk):
        here = slice(c * chunk, (c + 1) * chunk)
        pixels = lax.dot_general(
            both, table_ref[:, here], (((0,), (0,)), ((), ())), preferred_element_type=f32
        )
        mask = mask_ref[:, here].astype(f32)
        nqq, nqu, nuu = mask * qq_ref[:, here], mask * qu_ref[:, here], mask * uu_ref[:, here]
        parts = []
        for b in range(2):
            q = pixels[2 * b * cycles : (2 * b + 1) * cycles]
            u = pixels[(2 * b + 1) * cycles : (2 * b + 2) * cycles]
            parts += [nqq * q + nqu * u, nqu * q + nuu * u]
        weighted = jnp.concatenate(parts, axis=0).astype(bf16)
        part = lax.dot_general(
            table_ref[:top, here], weighted, (((1,), (1,)), ((), ())), preferred_element_type=f32
        )
        folded = part if folded is None else folded + part
    folded = jnp.concatenate([folded[:total_m], folded[total_m:]], axis=1)
    out = folded * cosine - pltpu.roll(folded, half, 1) * sine
    curve = jnp.sum(field * out, axis=0, keepdims=True)
    first_side = (lane_index(curve.shape) // (half // 2)) % 2 == 0
    curve = join_halves(jnp.where(first_side, curve, 0.0), jnp.where(first_side, 0.0, curve))
    for m in range(slots):
        for k in range(groups // ROWS):
            at = (m * (groups // ROWS) + k) * ROWS
            send_tile(send_ref, out[at : at + ROWS], m, k, sections, slots)

    prior = prior_rows(prior_ref)
    own = None
    for m in range(slots):
        d = d_ref[m]
        if not first:
            d = r_ref[m] + by_row(ratio, (ROWS, LANES))[:, :1] * d
            d_out[m] = d
        product = prior * d * d
        own = product if own is None else own + product

    send_scalars(send_ref, curve + row_totals(own), slots)


def prior_rows(prior_ref):
    e = prior_ref[0:1, :]
    b = prior_ref[1:2, :]
    shape = (ROWS, prior_ref.shape[1])
    return jnp.where((row_index(shape) >> 1) & 1 == 0, jnp.broadcast_to(e, shape), jnp.broadcast_to(b, shape))


def image_terms(recv_ref, buffer_ref, m, sections, cycles, slots):
    tiles = []
    for k in range(cycles // LANES):
        at = m * (cycles // LANES) + k
        tile = received_tile(recv_ref, m, k, sections, slots)
        tiles.append(to_rows(tile, buffer_ref.at[at]))
    field = jnp.concatenate(tiles, axis=1) if len(tiles) > 1 else tiles[0]
    return split_rows(jnp.concatenate([-field, flip_signed(field)], axis=1))


def next_residual(both, legendre_ref, r_ref, d_ref, m, alpha, prior):
    image = jnp.dot(both, legendre_ref[m], preferred_element_type=f32)
    image = (image[:ROWS] + image[ROWS:]) + prior * d_ref[m]
    return r_ref[m] - alpha * image


def step_size(recv_ref, rr_ref, slots):
    curve = pair(received_scalars(recv_ref, slots))
    two = tuple(a / b for a, b in zip(unspread(rr_ref[...]), curve))
    return by_row(two, (ROWS, LANES))[:, :1]


def update_kernel(
    sections, cycles, first, recv_ref, rr_ref, prior_ref, legendre_ref, r_ref, d_ref, turned_ref, *refs
):
    if not first:
        x_ref, *refs = refs
    send_ref, r_out, x_out, buffer_ref = refs
    slots = r_ref.shape[0]
    alpha = step_size(recv_ref, rr_ref, slots)
    prior = prior_rows(prior_ref)
    square = None
    terms = [image_terms(recv_ref, buffer_ref, m, sections, cycles, slots) for m in range(slots)]
    for m in range(slots):
        r = next_residual(terms[m], legendre_ref, r_ref, d_ref, m, alpha, prior)
        r_out[m] = r
        square = r * r if square is None else square + r * r
        forward_send(turned_product(r, turned_ref, m), send_ref, buffer_ref, m, sections, cycles, slots)
        x_out[m] = alpha * d_ref[m] if first else x_ref[m] + alpha * d_ref[m]
    send_scalars(send_ref, spread(pair(row_totals(square))), slots)


def last_kernel(
    sections,
    cycles,
    recv_ref,
    rr_ref,
    prior_ref,
    legendre_ref,
    r_ref,
    d_ref,
    x_ref,
    solution_ref,
    send_ref,
    residual_out,
    solution_out,
    buffer_ref,
):
    slots = r_ref.shape[0]
    alpha = step_size(recv_ref, rr_ref, slots)
    prior = prior_rows(prior_ref)
    for m in range(slots):
        x = x_ref[m] + alpha * d_ref[m]
        for b in range(2):
            solution_out[b, m] = solution_ref[b, m] + x[4 * b : 4 * b + 4]
    square = None
    terms = [image_terms(recv_ref, buffer_ref, m, sections, cycles, slots) for m in range(slots)]
    for m in range(slots):
        r = next_residual(terms[m], legendre_ref, r_ref, d_ref, m, alpha, prior)
        square = r * r if square is None else square + r * r
        for b in range(2):
            residual_out[b, m] = r[4 * b : 4 * b + 4]
    send_scalars(send_ref, row_totals(square), 0)


def end_kernel(
    recv_ref, rr_ref, d_ref, residual_ref, solution_ref, direction_hbm, residual_hbm, solution_hbm, direction_ref, sems
):
    slots = d_ref.shape[0]
    copies = [
        pltpu.make_async_copy(residual_ref, residual_hbm, sems.at[0]),
        pltpu.make_async_copy(solution_ref, solution_hbm, sems.at[1]),
        pltpu.make_async_copy(direction_ref, direction_hbm, sems.at[2]),
    ]
    copies[0].start()
    copies[1].start()
    before = unspread(rr_ref[...])
    now = pair(received_scalars(recv_ref, 0))
    ratios = [now[b] / before[b] for b in range(2)]

    def fill(m, carry):
        for b in range(2):
            direction_ref[b, m] = residual_ref[b, m] + ratios[b] * d_ref[m, 4 * b : 4 * b + 4]
        return carry

    lax.fori_loop(0, slots, fill, 0)
    copies[2].start()
    for copy in copies:
        copy.wait()


def call(kernel, outs, name, limit=24 << 20, hbm=(), scratch=(), hbm_outs=()):
    def run(*args):
        vmem = pl.BlockSpec(memory_space=pltpu.VMEM)
        specs = [vmem] * len(args)
        args = list(args)
        for i in hbm:
            specs[i] = pl.BlockSpec(memory_space=pltpu.HBM)
            args[i] = pltpu.with_memory_space_constraint(args[i], pltpu.HBM)
        return pl.pallas_call(
            kernel,
            out_shape=[jax.ShapeDtypeStruct(shape, dtype) for shape, dtype in outs],
            in_specs=specs,
            out_specs=[pl.BlockSpec(memory_space=pltpu.HBM) if i in hbm_outs else vmem for i in range(len(outs))],
            scratch_shapes=list(scratch),
            compiler_params=pltpu.CompilerParams(vmem_limit_bytes=limit),
            name=name,
        )(*args)

    return run


def per_device(
    solution_in,
    residual_in,
    direction_in,
    legendre,
    inverse_prior,
    noise_qq,
    noise_qu,
    noise_uu,
    pixel_mask,
    cycle_phase,
    m_values,
):
    sections = lax.axis_size("sec")
    devices = sections * lax.axis_size("grp")
    slots, cycles, length = legendre.shape[0], legendre.shape[2], legendre.shape[3]
    total_m = m_values.shape[0]
    count = noise_qq.shape[1]
    message = ((devices * (slots + 1), LANES), f32)
    scalars = ((devices, LANES), f32)
    inner = ((slots, ROWS, length), f32)
    outer = (solution_in.shape, f32)
    vector = ((1, LANES), f32)
    field_like = ((total_m, LANES), f32)
    chunk = min(256, count)

    buffers = (pltpu.VMEM((slots * (cycles // LANES), 10 * ROWS, LANES), f32),)

    def exchange(x):
        blocks = x.reshape(devices, 1, x.size // devices)
        return lax.all_to_all(blocks, ("sec", "grp"), 0, 0, tiled=True).reshape(x.shape)

    table = ((4 * total_m, count), bf16)
    blocks = ((slots, 2 * cycles, length), bf16)
    turned_blocks = ((slots, length, 2 * cycles), bf16)
    send, trig, cosine, sine, rows, r, d = call(
        functools.partial(start_kernel, sections, cycles),
        [message, table, field_like, field_like, blocks, inner, inner],
        "start",
        hbm=range(5),
        scratch=(
            pltpu.SMEM((total_m,), jnp.int32),
            pltpu.VMEM((cycle_phase.shape[0] // LANES, LANES), f32),
            pltpu.VMEM(residual_in.shape, f32),
            pltpu.VMEM(direction_in.shape, f32),
            *buffers,
            pltpu.SemaphoreType.DMA((2,)),
            pltpu.SemaphoreType.DMA((2,)),
            pltpu.SemaphoreType.DMA((slots,)),
        ),
    )(m_values, cycle_phase.reshape(-1, LANES), residual_in, direction_in, legendre.reshape(blocks[0]))
    noise = (noise_qq, noise_qu, noise_uu, pixel_mask)
    for step in range(ITERS):
        first, last = step == 0, step == ITERS - 1
        recv = exchange(send)
        carried = (rows,) if first else (r, field, rr)
        out = call(
            functools.partial(pixel_kernel, sections, chunk, first, last),
            [message, vector] + [turned_blocks if first else inner] + ([] if last else [field_like]),
            "pixels",
        )(recv, trig, cosine, sine, *noise, inverse_prior, d, *carried)
        send, rr, *out = out
        if first:
            turned, *out = out
        else:
            d, *out = out
        if not last:
            (field,) = out
        recv = exchange(send)
        carried = (recv, rr, inverse_prior, rows, r, d) + (() if last else (turned,)) + (() if first else (x,))
        if last:
            send, residual, solution = call(
                functools.partial(last_kernel, sections, cycles),
                [scalars, outer, outer],
                "last",
                scratch=buffers,
            )(*carried, solution_in)
        else:
            send, r, x = call(
                functools.partial(update_kernel, sections, cycles, first), [message, inner, inner], "update", scratch=buffers
            )(*carried)
    recv = exchange(send)
    direction, residual, solution = call(
        end_kernel,
        [outer, outer, outer],
        "end",
        hbm_outs=(0, 1, 2),
        scratch=(pltpu.VMEM(outer[0], f32), pltpu.SemaphoreType.DMA((3,))),
    )(recv, rr, d, residual, solution)
    return solution, residual, direction


def solution(mesh):
    return jax.shard_map(
        per_device,
        mesh=mesh,
        in_specs=(
            P(None, "grp", None, "sec"),
            P(None, "grp", None, "sec"),
            P(None, "grp", None, "sec"),
            P("grp", None, None, "sec"),
            P(None, "sec"),
            P("grp", "sec"),
            P("grp", "sec"),
            P("grp", "sec"),
            P("grp", "sec"),
            P(),
            P(),
        ),
        out_specs=(
            P(None, "grp", None, "sec"),
            P(None, "grp", None, "sec"),
            P(None, "grp", None, "sec"),
        ),
        check_vma=False,
    )
```

```python
import functools
import math

import jax
import jax.numpy as jnp
from jax import lax
from jax.experimental import pallas as pl
from jax.experimental.pallas import tpu as pltpu
from jax.sharding import PartitionSpec as P

ITERS = 4
LANES = 128
ROWS = 8
full_turn = 2.0 * math.pi
f32 = jnp.float32
bf16 = jnp.bfloat16

flipped = tuple(n ^ 3 for n in range(ROWS))


def row_index(shape):
    return lax.broadcasted_iota(jnp.int32, shape, 0)


def lane_index(shape):
    return lax.broadcasted_iota(jnp.int32, shape, 1)


def permute_rows(x, order):
    rows = row_index(x.shape)
    by_shift = {}
    for t, n in enumerate(order):
        by_shift.setdefault((t - n) % ROWS, []).append(t)
    out = None
    for shift, targets in by_shift.items():
        moved = pltpu.roll(x, shift, 0) if shift else x
        if out is None:
            out = moved
        else:
            mask = functools.reduce(jnp.logical_or, [rows == t for t in targets])
            out = jnp.where(mask, moved, out)
    return out


def turn_blocks(buffer_ref, start, stride, distance):
    width = LANES // ROWS
    out = None
    for k in range(ROWS):
        moved = buffer_ref[pl.ds(start + 4 * k, ROWS, stride=stride), :]
        out = moved if out is None else jnp.where(distance == k, pltpu.roll(moved, k * width, 1), out)
    return out


def store_copies(x, buffer_ref, starts, stride):
    for start in starts:
        buffer_ref[pl.ds(start, ROWS, stride=stride), :] = x


def to_rows(x, buffer_ref):
    store_copies(x, buffer_ref, (16, 48, 2, 34), 4)
    rows = row_index(x.shape)
    place = (rows & 1) * 4 + (rows >> 1)
    distance = (lane_index(x.shape) // (LANES // ROWS) - place) & (ROWS - 1)
    return turn_blocks(buffer_ref, 16, 2, distance)


def to_message(x, buffer_ref):
    store_copies(x, buffer_ref, (0, 14, 32, 46), 2)
    distance = (lane_index(x.shape) // (LANES // ROWS) - row_index(x.shape)) & (ROWS - 1)
    return turn_blocks(buffer_ref, 0, 4, distance)


def split_rows(x):
    high = x.astype(bf16).astype(f32)
    return jnp.concatenate([high, x - high], axis=0).astype(bf16)


def flip_signed(x):
    rows = row_index(x.shape)
    same = ((rows >> 1) & 1) == (rows & 1)
    moved = permute_rows(x, flipped)
    return jnp.where(same, moved, -moved)


def row_totals(x):
    tile = x[:, :LANES]
    for k in range(1, x.shape[1] // LANES):
        tile = tile + x[:, k * LANES : (k + 1) * LANES]
    rows = row_index(tile.shape)
    first = jnp.sum(jnp.where(rows < 4, tile, 0.0), axis=0, keepdims=True)
    second = jnp.sum(jnp.where(rows < 4, 0.0, tile), axis=0, keepdims=True)
    return join_halves(first, second)


def join_halves(first, second):
    first = first + pltpu.roll(first, LANES // 2, 1)
    second = second + pltpu.roll(second, LANES // 2, 1)
    return jnp.where(lane_index(first.shape) < LANES // 2, first, second)


def pair(vector):
    low = lane_index(vector.shape) < LANES // 2
    return (
        jnp.sum(jnp.where(low, vector, 0.0), axis=1, keepdims=True),
        jnp.sum(jnp.where(low, 0.0, vector), axis=1, keepdims=True),
    )


def spread(two):
    return by_lane(two, (1, LANES))


def unspread(vector):
    spot = lane_index(vector.shape)
    return [jnp.sum(jnp.where(spot == b * (LANES // 4), vector, 0.0), axis=1, keepdims=True) for b in range(2)]


def by_row(two, shape):
    return jnp.where(row_index(shape) < 4, two[0], two[1])


def by_lane(two, shape):
    quarter = LANES // 4
    return jnp.where((lane_index(shape) // quarter) % 2 == 0, two[0], two[1])


def forward_product(values, legendre_ref, m):
    return lax.dot_general(
        split_rows(values),
        legendre_ref[m],
        (((1,), (1,)), ((), ())),
        preferred_element_type=f32,
    )


def turned_product(values, turned_ref, m):
    return jnp.dot(split_rows(values), turned_ref[m], preferred_element_type=f32)


def forward_send(prod, send_ref, buffer_ref, m, sections, cycles, slots):
    prod = prod[:ROWS] + prod[ROWS:]
    field = flip_signed(prod[:, cycles:]) - prod[:, :cycles]
    for k in range(cycles // LANES):
        tile = field[:, k * LANES : (k + 1) * LANES]
        at = m * (cycles // LANES) + k
        send_tile(send_ref, to_message(tile, buffer_ref.at[at]), m, k, sections, slots)


def tile_rows(ref, m, k, s, sections, slots):
    groups = ref.shape[0] // (slots + 1) // sections
    return pl.ds((s * groups + k * ROWS) * (slots + 1) + m, ROWS, stride=slots + 1)


def send_tile(send_ref, tile, m, k, sections, slots):
    for s in range(sections):
        send_ref[tile_rows(send_ref, m, k, s, sections, slots), :] = tile


def scalar_rows(ref, slots):
    count = ref.shape[0] // (slots + 1)
    return pl.ds(slots, count, stride=slots + 1) if slots else slice(None)


def send_scalars(send_ref, vector, slots):
    count = send_ref.shape[0] // (slots + 1)
    send_ref[scalar_rows(send_ref, slots), :] = jnp.broadcast_to(vector, (count, LANES))


def received_scalars(recv_ref, slots):
    return jnp.sum(recv_ref[scalar_rows(recv_ref, slots), :], axis=0, keepdims=True)


def received_tile(recv_ref, m, k, sections, slots):
    total = None
    for s in range(sections):
        part = recv_ref[tile_rows(recv_ref, m, k, s, sections, slots), :]
        total = part if total is None else total + part
    return total


def fill_tables(slots, total, m_ref, phase_ref, table_ref, cos_ref, sin_ref):
    total_m = cos_ref.shape[0]
    count = table_ref.shape[1]
    groups = total_m // slots
    rows = row_index((ROWS, LANES))
    columns = []
    for m in range(slots):
        for k in range(groups // ROWS):
            column = jnp.zeros((ROWS, LANES), jnp.int32)
            for i in range(ROWS):
                column = jnp.where(rows == i, m_ref[(k * ROWS + i) * slots + m], column)
            columns.append(column)
    column = jnp.concatenate(columns, axis=0)
    value = column.astype(f32)
    weight = jnp.where(column == 0, 1.0, 2.0).astype(f32)
    lanes = lane_index(column.shape)

    me = lax.axis_index("grp")
    width = LANES // ROWS
    phases = phase_ref[pl.ds(me // ROWS, 1), :]
    spot = lane_index(phases.shape)
    moved = pltpu.roll(phases, (ROWS - me % ROWS) % ROWS * width, 1)
    local = jnp.where(spot < width, moved, 0.0)
    for k in (1, 2, 4):
        local = local + pltpu.roll(local, k * width, 1)
    turn = value * local
    cosine = jnp.cos(turn)
    sine = jnp.sin(turn)
    cos_ref[...] = cosine
    sin_ref[...] = jnp.where(lanes < LANES // 2, -sine, sine)

    def wrap(index):
        return index & (total - 1) if total & (total - 1) == 0 else index % total

    step = full_turn / total
    start = lax.axis_index("sec") * count
    fine = wrap(column * lanes).astype(f32) * step
    coarse = wrap(column * (start + lanes * LANES)).astype(f32) * step
    fine_cos, fine_sin = jnp.cos(fine), jnp.sin(fine)
    coarse_cos, coarse_sin = weight * jnp.cos(coarse), weight * jnp.sin(coarse)
    for a in range(count // LANES):
        cos_a = coarse_cos[:, a : a + 1]
        sin_a = coarse_sin[:, a : a + 1]
        block = jnp.concatenate([cos_a * fine_cos - sin_a * fine_sin, -(sin_a * fine_cos + cos_a * fine_sin)], axis=0)
        block = block.astype(bf16)
        here = slice(a * LANES, (a + 1) * LANES)
        table_ref[: 2 * total_m, here] = block
        table_ref[2 * total_m :, here] = block


def start_kernel(
    sections,
    cycles,
    m_hbm,
    phase_hbm,
    residual_hbm,
    direction_hbm,
    legendre_hbm,
    send_ref,
    table_ref,
    cos_ref,
    sin_ref,
    legendre_ref,
    r_ref,
    d_ref,
    m_ref,
    phase_ref,
    residual_ref,
    direction_ref,
    buffer_ref,
    small_sems,
    value_sems,
    legendre_sems,
):
    slots = r_ref.shape[0]
    small = [
        pltpu.make_async_copy(m_hbm, m_ref, small_sems.at[0]),
        pltpu.make_async_copy(phase_hbm, phase_ref, small_sems.at[1]),
    ]
    for copy in small:
        copy.start()
    copies = [
        pltpu.make_async_copy(direction_hbm, direction_ref, value_sems.at[0]),
        pltpu.make_async_copy(residual_hbm, residual_ref, value_sems.at[1]),
    ]
    blocks = [
        pltpu.make_async_copy(legendre_hbm.at[m], legendre_ref.at[m], legendre_sems.at[m]) for m in range(slots)
    ]
    for copy in copies:
        copy.start()
    for block in blocks:
        block.start()
    for copy in small:
        copy.wait()
    fill_tables(slots, table_ref.shape[1] * sections, m_ref, phase_ref, table_ref, cos_ref, sin_ref)
    copies[0].wait()
    rows = []
    for m in range(slots):
        d = jnp.concatenate([direction_ref[0, m], direction_ref[1, m]], axis=0)
        d_ref[m] = d
        rows.append(d)
    copies[1].wait()
    square = None
    for m in range(slots):
        r = jnp.concatenate([residual_ref[0, m], residual_ref[1, m]], axis=0)
        r_ref[m] = r
        square = r * r if square is None else square + r * r
    send_scalars(send_ref, spread(pair(row_totals(square))), slots)
    for block in blocks:
        block.wait()
    for m in range(slots):
        forward_send(forward_product(rows[m], legendre_ref, m), send_ref, buffer_ref, m, sections, cycles, slots)


def pixel_kernel(
    sections,
    chunk,
    first,
    last,
    recv_ref,
    table_ref,
    cos_ref,
    sin_ref,
    qq_ref,
    qu_ref,
    uu_ref,
    mask_ref,
    prior_ref,
    d_ref,
    *refs,
):
    if first:
        legendre_ref, *refs = refs
    else:
        r_ref, field_ref, rr_ref, *refs = refs
    send_ref, rr_out, *refs = refs
    if first:
        turned_ref, *refs = refs
    if not first:
        d_out, *refs = refs
    if not last:
        (field_out,) = refs
    total_m = cos_ref.shape[0]
    slots = d_ref.shape[0]
    groups = total_m // slots
    tiles = [received_tile(recv_ref, m, k, sections, slots) for m in range(slots) for k in range(groups // ROWS)]
    field = jnp.concatenate(tiles, axis=0)
    scalars = received_scalars(recv_ref, slots)
    rr_out[...] = scalars
    if not first:
        lane_ratio = scalars / rr_ref[...]
        ratio = unspread(lane_ratio)
        field = field + lane_ratio * field_ref[...]
    if not last:
        field_out[...] = field
    half = LANES // 2
    cosine, sine = cos_ref[...], sin_ref[...]
    turned = field * cosine + pltpu.roll(field, half, 1) * sine
    modes = jnp.concatenate([turned[:, :half], turned[:, half:]], axis=0)
    high = modes.astype(bf16).astype(f32)
    both = jnp.concatenate([high, modes - high], axis=0).astype(bf16)
    count = qq_ref.shape[1]
    cycles = qq_ref.shape[0]
    top = 2 * total_m
    folded = None
    for c in range(count // chunk):
        here = slice(c * chunk, (c + 1) * chunk)
        pixels = lax.dot_general(
            both, table_ref[:, here], (((0,), (0,)), ((), ())), preferred_element_type=f32
        )
        mask = mask_ref[:, here].astype(f32)
        nqq, nqu, nuu = mask * qq_ref[:, here], mask * qu_ref[:, here], mask * uu_ref[:, here]
        parts = []
        for b in range(2):
            q = pixels[2 * b * cycles : (2 * b + 1) * cycles]
            u = pixels[(2 * b + 1) * cycles : (2 * b + 2) * cycles]
            parts += [nqq * q + nqu * u, nqu * q + nuu * u]
        weighted = jnp.concatenate(parts, axis=0).astype(bf16)
        part = lax.dot_general(
            table_ref[:top, here], weighted, (((1,), (1,)), ((), ())), preferred_element_type=f32
        )
        folded = part if folded is None else folded + part
    folded = jnp.concatenate([folded[:total_m], folded[total_m:]], axis=1)
    out = folded * cosine - pltpu.roll(folded, half, 1) * sine
    curve = jnp.sum(field * out, axis=0, keepdims=True)
    first_side = (lane_index(curve.shape) // (half // 2)) % 2 == 0
    curve = join_halves(jnp.where(first_side, curve, 0.0), jnp.where(first_side, 0.0, curve))
    for m in range(slots):
        for k in range(groups // ROWS):
            at = (m * (groups // ROWS) + k) * ROWS
            send_tile(send_ref, out[at : at + ROWS], m, k, sections, slots)

    prior = prior_rows(prior_ref)
    own = None
    for m in range(slots):
        d = d_ref[m]
        if not first:
            d = r_ref[m] + by_row(ratio, (ROWS, LANES))[:, :1] * d
            d_out[m] = d
        product = prior * d * d
        own = product if own is None else own + product

    if first:
        for m in range(slots):
            turned_ref[m] = legendre_ref[m].T
    send_scalars(send_ref, curve + row_totals(own), slots)


def prior_rows(prior_ref):
    e = prior_ref[0:1, :]
    b = prior_ref[1:2, :]
    shape = (ROWS, prior_ref.shape[1])
    return jnp.where((row_index(shape) >> 1) & 1 == 0, jnp.broadcast_to(e, shape), jnp.broadcast_to(b, shape))


def image_terms(recv_ref, buffer_ref, m, sections, cycles, slots):
    tiles = []
    for k in range(cycles // LANES):
        at = m * (cycles // LANES) + k
        tile = received_tile(recv_ref, m, k, sections, slots)
        tiles.append(to_rows(tile, buffer_ref.at[at]))
    field = jnp.concatenate(tiles, axis=1) if len(tiles) > 1 else tiles[0]
    return split_rows(jnp.concatenate([-field, flip_signed(field)], axis=1))


def next_residual(both, legendre_ref, r_ref, d_ref, m, alpha, prior):
    image = jnp.dot(both, legendre_ref[m], preferred_element_type=f32)
    image = (image[:ROWS] + image[ROWS:]) + prior * d_ref[m]
    return r_ref[m] - alpha * image


def step_size(recv_ref, rr_ref, slots):
    curve = pair(received_scalars(recv_ref, slots))
    two = tuple(a / b for a, b in zip(unspread(rr_ref[...]), curve))
    return by_row(two, (ROWS, LANES))[:, :1]


def update_kernel(
    sections, cycles, first, recv_ref, rr_ref, prior_ref, legendre_ref, r_ref, d_ref, turned_ref, *refs
):
    if not first:
        x_ref, *refs = refs
    send_ref, r_out, x_out, buffer_ref = refs
    slots = r_ref.shape[0]
    alpha = step_size(recv_ref, rr_ref, slots)
    prior = prior_rows(prior_ref)
    square = None
    terms = [image_terms(recv_ref, buffer_ref, m, sections, cycles, slots) for m in range(slots)]
    waiting = None
    for m in range(slots + 1):
        if m < slots:
            r = next_residual(terms[m], legendre_ref, r_ref, d_ref, m, alpha, prior)
            r_out[m] = r
            square = r * r if square is None else square + r * r
            x_out[m] = alpha * d_ref[m] if first else x_ref[m] + alpha * d_ref[m]
        if waiting is not None:
            forward_send(turned_product(waiting, turned_ref, m - 1), send_ref, buffer_ref, m - 1, sections, cycles, slots)
        waiting = r
    send_scalars(send_ref, spread(pair(row_totals(square))), slots)


def last_kernel(
    sections,
    cycles,
    recv_ref,
    rr_ref,
    prior_ref,
    legendre_ref,
    r_ref,
    d_ref,
    x_ref,
    solution_ref,
    send_ref,
    residual_out,
    solution_out,
    buffer_ref,
):
    slots = r_ref.shape[0]
    alpha = step_size(recv_ref, rr_ref, slots)
    prior = prior_rows(prior_ref)
    for m in range(slots):
        x = x_ref[m] + alpha * d_ref[m]
        for b in range(2):
            solution_out[b, m] = solution_ref[b, m] + x[4 * b : 4 * b + 4]
    square = None
    terms = [image_terms(recv_ref, buffer_ref, m, sections, cycles, slots) for m in range(slots)]
    for m in range(slots):
        r = next_residual(terms[m], legendre_ref, r_ref, d_ref, m, alpha, prior)
        square = r * r if square is None else square + r * r
        for b in range(2):
            residual_out[b, m] = r[4 * b : 4 * b + 4]
    send_scalars(send_ref, row_totals(square), 0)


def end_kernel(
    recv_ref, rr_ref, d_ref, residual_ref, solution_ref, direction_hbm, residual_hbm, solution_hbm, direction_ref, sems
):
    slots = d_ref.shape[0]
    copies = [
        pltpu.make_async_copy(residual_ref, residual_hbm, sems.at[0]),
        pltpu.make_async_copy(solution_ref, solution_hbm, sems.at[1]),
        pltpu.make_async_copy(direction_ref, direction_hbm, sems.at[2]),
    ]
    copies[0].start()
    copies[1].start()
    before = unspread(rr_ref[...])
    now = pair(received_scalars(recv_ref, 0))
    ratios = [now[b] / before[b] for b in range(2)]

    def fill(m, carry):
        for b in range(2):
            direction_ref[b, m] = residual_ref[b, m] + ratios[b] * d_ref[m, 4 * b : 4 * b + 4]
        return carry

    lax.fori_loop(0, slots, fill, 0)
    copies[2].start()
    for copy in copies:
        copy.wait()


def call(kernel, outs, name, limit=24 << 20, hbm=(), scratch=(), hbm_outs=()):
    def run(*args):
        vmem = pl.BlockSpec(memory_space=pltpu.VMEM)
        specs = [vmem] * len(args)
        args = list(args)
        for i in hbm:
            specs[i] = pl.BlockSpec(memory_space=pltpu.HBM)
            args[i] = pltpu.with_memory_space_constraint(args[i], pltpu.HBM)
        return pl.pallas_call(
            kernel,
            out_shape=[jax.ShapeDtypeStruct(shape, dtype) for shape, dtype in outs],
            in_specs=specs,
            out_specs=[pl.BlockSpec(memory_space=pltpu.HBM) if i in hbm_outs else vmem for i in range(len(outs))],
            scratch_shapes=list(scratch),
            compiler_params=pltpu.CompilerParams(vmem_limit_bytes=limit),
            name=name,
        )(*args)

    return run


def per_device(
    solution_in,
    residual_in,
    direction_in,
    legendre,
    inverse_prior,
    noise_qq,
    noise_qu,
    noise_uu,
    pixel_mask,
    cycle_phase,
    m_values,
):
    sections = lax.axis_size("sec")
    devices = sections * lax.axis_size("grp")
    slots, cycles, length = legendre.shape[0], legendre.shape[2], legendre.shape[3]
    total_m = m_values.shape[0]
    count = noise_qq.shape[1]
    message = ((devices * (slots + 1), LANES), f32)
    scalars = ((devices, LANES), f32)
    inner = ((slots, ROWS, length), f32)
    outer = (solution_in.shape, f32)
    vector = ((1, LANES), f32)
    field_like = ((total_m, LANES), f32)
    chunk = min(256, count)

    buffers = (pltpu.VMEM((slots * (cycles // LANES), 10 * ROWS, LANES), f32),)

    def exchange(x):
        blocks = x.reshape(devices, 1, x.size // devices)
        return lax.all_to_all(blocks, ("sec", "grp"), 0, 0, tiled=True).reshape(x.shape)

    table = ((4 * total_m, count), bf16)
    blocks = ((slots, 2 * cycles, length), bf16)
    turned_blocks = ((slots, length, 2 * cycles), bf16)
    send, trig, cosine, sine, rows, r, d = call(
        functools.partial(start_kernel, sections, cycles),
        [message, table, field_like, field_like, blocks, inner, inner],
        "start",
        hbm=range(5),
        scratch=(
            pltpu.SMEM((total_m,), jnp.int32),
            pltpu.VMEM((cycle_phase.shape[0] // LANES, LANES), f32),
            pltpu.VMEM(residual_in.shape, f32),
            pltpu.VMEM(direction_in.shape, f32),
            *buffers,
            pltpu.SemaphoreType.DMA((2,)),
            pltpu.SemaphoreType.DMA((2,)),
            pltpu.SemaphoreType.DMA((slots,)),
        ),
    )(m_values, cycle_phase.reshape(-1, LANES), residual_in, direction_in, legendre.reshape(blocks[0]))
    noise = (noise_qq, noise_qu, noise_uu, pixel_mask)
    for step in range(ITERS):
        first, last = step == 0, step == ITERS - 1
        recv = exchange(send)
        carried = (rows,) if first else (r, field, rr)
        out = call(
            functools.partial(pixel_kernel, sections, chunk, first, last),
            [message, vector] + [turned_blocks if first else inner] + ([] if last else [field_like]),
            "pixels",
        )(recv, trig, cosine, sine, *noise, inverse_prior, d, *carried)
        send, rr, *out = out
        if first:
            turned, *out = out
        else:
            d, *out = out
        if not last:
            (field,) = out
        recv = exchange(send)
        carried = (recv, rr, inverse_prior, rows, r, d) + (() if last else (turned,)) + (() if first else (x,))
        if last:
            send, residual, solution = call(
                functools.partial(last_kernel, sections, cycles),
                [scalars, outer, outer],
                "last",
                scratch=buffers,
            )(*carried, solution_in)
        else:
            send, r, x = call(
                functools.partial(update_kernel, sections, cycles, first), [message, inner, inner], "update", scratch=buffers
            )(*carried)
    recv = exchange(send)
    direction, residual, solution = call(
        end_kernel,
        [outer, outer, outer],
        "end",
        hbm_outs=(0, 1, 2),
        scratch=(pltpu.VMEM(outer[0], f32), pltpu.SemaphoreType.DMA((3,))),
    )(recv, rr, d, residual, solution)
    return solution, residual, direction


def solution(mesh):
    return jax.shard_map(
        per_device,
        mesh=mesh,
        in_specs=(
            P(None, "grp", None, "sec"),
            P(None, "grp", None, "sec"),
            P(None, "grp", None, "sec"),
            P("grp", None, None, "sec"),
            P(None, "sec"),
            P("grp", "sec"),
            P("grp", "sec"),
            P("grp", "sec"),
            P("grp", "sec"),
            P(),
            P(),
        ),
        out_specs=(
            P(None, "grp", None, "sec"),
            P(None, "grp", None, "sec"),
            P(None, "grp", None, "sec"),
        ),
        check_vma=False,
    )
```

```python
import functools
import math

import jax
import jax.numpy as jnp
from jax import lax
from jax.experimental import pallas as pl
from jax.experimental.pallas import tpu as pltpu
from jax.sharding import PartitionSpec as P

ITERS = 4
LANES = 128
ROWS = 8
full_turn = 2.0 * math.pi
f32 = jnp.float32
bf16 = jnp.bfloat16

flipped = tuple(n ^ 3 for n in range(ROWS))


def row_index(shape):
    return lax.broadcasted_iota(jnp.int32, shape, 0)


def lane_index(shape):
    return lax.broadcasted_iota(jnp.int32, shape, 1)


def permute_rows(x, order):
    rows = row_index(x.shape)
    by_shift = {}
    for t, n in enumerate(order):
        by_shift.setdefault((t - n) % ROWS, []).append(t)
    out = None
    for shift, targets in by_shift.items():
        moved = pltpu.roll(x, shift, 0) if shift else x
        if out is None:
            out = moved
        else:
            mask = functools.reduce(jnp.logical_or, [rows == t for t in targets])
            out = jnp.where(mask, moved, out)
    return out


def turn_blocks(buffer_ref, start, stride, distance):
    width = LANES // ROWS
    out = None
    for k in range(ROWS):
        moved = buffer_ref[pl.ds(start + 4 * k, ROWS, stride=stride), :]
        out = moved if out is None else jnp.where(distance == k, pltpu.roll(moved, k * width, 1), out)
    return out


def store_copies(x, buffer_ref, starts, stride):
    for start in starts:
        buffer_ref[pl.ds(start, ROWS, stride=stride), :] = x


def to_rows(x, buffer_ref):
    store_copies(x, buffer_ref, (16, 48, 2, 34), 4)
    rows = row_index(x.shape)
    place = (rows & 1) * 4 + (rows >> 1)
    distance = (lane_index(x.shape) // (LANES // ROWS) - place) & (ROWS - 1)
    return turn_blocks(buffer_ref, 16, 2, distance)


def to_message(x, buffer_ref):
    store_copies(x, buffer_ref, (0, 14, 32, 46), 2)
    distance = (lane_index(x.shape) // (LANES // ROWS) - row_index(x.shape)) & (ROWS - 1)
    return turn_blocks(buffer_ref, 0, 4, distance)


def split_rows(x):
    high = x.astype(bf16).astype(f32)
    return jnp.concatenate([high, x - high], axis=0).astype(bf16)


def flip_signed(x):
    rows = row_index(x.shape)
    same = ((rows >> 1) & 1) == (rows & 1)
    moved = permute_rows(x, flipped)
    return jnp.where(same, moved, -moved)


def row_totals(x):
    tile = x[:, :LANES]
    for k in range(1, x.shape[1] // LANES):
        tile = tile + x[:, k * LANES : (k + 1) * LANES]
    rows = row_index(tile.shape)
    first = jnp.sum(jnp.where(rows < 4, tile, 0.0), axis=0, keepdims=True)
    second = jnp.sum(jnp.where(rows < 4, 0.0, tile), axis=0, keepdims=True)
    return join_halves(first, second)


def join_halves(first, second):
    first = first + pltpu.roll(first, LANES // 2, 1)
    second = second + pltpu.roll(second, LANES // 2, 1)
    return jnp.where(lane_index(first.shape) < LANES // 2, first, second)


def pair(vector):
    low = lane_index(vector.shape) < LANES // 2
    return (
        jnp.sum(jnp.where(low, vector, 0.0), axis=1, keepdims=True),
        jnp.sum(jnp.where(low, 0.0, vector), axis=1, keepdims=True),
    )


def spread(two):
    return by_lane(two, (1, LANES))


def unspread(vector):
    spot = lane_index(vector.shape)
    return [jnp.sum(jnp.where(spot == b * (LANES // 4), vector, 0.0), axis=1, keepdims=True) for b in range(2)]


def by_row(two, shape):
    return jnp.where(row_index(shape) < 4, two[0], two[1])


def by_lane(two, shape):
    quarter = LANES // 4
    return jnp.where((lane_index(shape) // quarter) % 2 == 0, two[0], two[1])


def forward_product(values, legendre_ref, m):
    return lax.dot_general(
        split_rows(values),
        legendre_ref[m],
        (((1,), (1,)), ((), ())),
        preferred_element_type=f32,
    )


def turned_product(values, turned_ref, m):
    return jnp.dot(split_rows(values), turned_ref[m], preferred_element_type=f32)


def forward_send(prod, send_ref, buffer_ref, m, sections, cycles, slots):
    prod = prod[:ROWS] + prod[ROWS:]
    field = flip_signed(prod[:, cycles:]) - prod[:, :cycles]
    for k in range(cycles // LANES):
        tile = field[:, k * LANES : (k + 1) * LANES]
        at = m * (cycles // LANES) + k
        send_tile(send_ref, to_message(tile, buffer_ref.at[at]), m, k, sections, slots)


def tile_rows(ref, m, k, s, sections, slots):
    groups = ref.shape[0] // (slots + 1) // sections
    return pl.ds((s * groups + k * ROWS) * (slots + 1) + m, ROWS, stride=slots + 1)


def send_tile(send_ref, tile, m, k, sections, slots):
    for s in range(sections):
        send_ref[tile_rows(send_ref, m, k, s, sections, slots), :] = tile


def scalar_rows(ref, slots):
    count = ref.shape[0] // (slots + 1)
    return pl.ds(slots, count, stride=slots + 1) if slots else slice(None)


def send_scalars(send_ref, vector, slots):
    count = send_ref.shape[0] // (slots + 1)
    send_ref[scalar_rows(send_ref, slots), :] = jnp.broadcast_to(vector, (count, LANES))


def received_scalars(recv_ref, slots):
    return jnp.sum(recv_ref[scalar_rows(recv_ref, slots), :], axis=0, keepdims=True)


def received_tile(recv_ref, m, k, sections, slots):
    total = None
    for s in range(sections):
        part = recv_ref[tile_rows(recv_ref, m, k, s, sections, slots), :]
        total = part if total is None else total + part
    return total


def fill_tables(slots, total, m_ref, phase_ref, table_ref, cos_ref, sin_ref):
    total_m = cos_ref.shape[0]
    count = table_ref.shape[1]
    groups = total_m // slots
    rows = row_index((ROWS, LANES))
    columns = []
    for m in range(slots):
        for k in range(groups // ROWS):
            column = jnp.zeros((ROWS, LANES), jnp.int32)
            for i in range(ROWS):
                column = jnp.where(rows == i, m_ref[(k * ROWS + i) * slots + m], column)
            columns.append(column)
    column = jnp.concatenate(columns, axis=0)
    value = column.astype(f32)
    weight = jnp.where(column == 0, 1.0, 2.0).astype(f32)
    lanes = lane_index(column.shape)

    me = lax.axis_index("grp")
    width = LANES // ROWS
    phases = phase_ref[pl.ds(me // ROWS, 1), :]
    spot = lane_index(phases.shape)
    moved = pltpu.roll(phases, (ROWS - me % ROWS) % ROWS * width, 1)
    local = jnp.where(spot < width, moved, 0.0)
    for k in (1, 2, 4):
        local = local + pltpu.roll(local, k * width, 1)
    turn = value * local
    cosine = jnp.cos(turn)
    sine = jnp.sin(turn)
    cos_ref[...] = cosine
    sin_ref[...] = jnp.where(lanes < LANES // 2, -sine, sine)

    def wrap(index):
        return index & (total - 1) if total & (total - 1) == 0 else index % total

    step = full_turn / total
    start = lax.axis_index("sec") * count
    fine = wrap(column * lanes).astype(f32) * step
    coarse = wrap(column * (start + lanes * LANES)).astype(f32) * step
    fine_cos, fine_sin = jnp.cos(fine), jnp.sin(fine)
    coarse_cos, coarse_sin = weight * jnp.cos(coarse), weight * jnp.sin(coarse)
    for a in range(count // LANES):
        cos_a = coarse_cos[:, a : a + 1]
        sin_a = coarse_sin[:, a : a + 1]
        block = jnp.concatenate([cos_a * fine_cos - sin_a * fine_sin, -(sin_a * fine_cos + cos_a * fine_sin)], axis=0)
        block = block.astype(bf16)
        here = slice(a * LANES, (a + 1) * LANES)
        table_ref[: 2 * total_m, here] = block
        table_ref[2 * total_m :, here] = block


def start_kernel(
    sections,
    cycles,
    m_hbm,
    phase_hbm,
    residual_hbm,
    direction_hbm,
    legendre_hbm,
    send_ref,
    table_ref,
    cos_ref,
    sin_ref,
    legendre_ref,
    r_ref,
    d_ref,
    m_ref,
    phase_ref,
    residual_ref,
    direction_ref,
    buffer_ref,
    small_sems,
    value_sems,
    legendre_sems,
):
    slots = r_ref.shape[0]
    small = [
        pltpu.make_async_copy(m_hbm, m_ref, small_sems.at[0]),
        pltpu.make_async_copy(phase_hbm, phase_ref, small_sems.at[1]),
    ]
    for copy in small:
        copy.start()
    copies = [
        pltpu.make_async_copy(direction_hbm, direction_ref, value_sems.at[0]),
        pltpu.make_async_copy(residual_hbm, residual_ref, value_sems.at[1]),
    ]
    blocks = [
        pltpu.make_async_copy(legendre_hbm.at[m], legendre_ref.at[m], legendre_sems.at[m]) for m in range(slots)
    ]
    for copy in copies:
        copy.start()
    for block in blocks:
        block.start()
    for copy in small:
        copy.wait()
    fill_tables(slots, table_ref.shape[1] * sections, m_ref, phase_ref, table_ref, cos_ref, sin_ref)
    copies[0].wait()
    rows = []
    for m in range(slots):
        d = jnp.concatenate([direction_ref[0, m], direction_ref[1, m]], axis=0)
        d_ref[m] = d
        rows.append(d)
    copies[1].wait()
    square = None
    for m in range(slots):
        r = jnp.concatenate([residual_ref[0, m], residual_ref[1, m]], axis=0)
        r_ref[m] = r
        square = r * r if square is None else square + r * r
    send_scalars(send_ref, spread(pair(row_totals(square))), slots)
    for block in blocks:
        block.wait()
    for m in range(slots):
        forward_send(forward_product(rows[m], legendre_ref, m), send_ref, buffer_ref, m, sections, cycles, slots)


def pixel_kernel(
    sections,
    chunk,
    first,
    last,
    recv_ref,
    table_ref,
    cos_ref,
    sin_ref,
    qq_ref,
    qu_ref,
    uu_ref,
    mask_ref,
    prior_ref,
    d_ref,
    *refs,
):
    if first:
        legendre_ref, *refs = refs
    else:
        r_ref, field_ref, rr_ref, *refs = refs
    send_ref, rr_out, *refs = refs
    if first:
        turned_ref, *refs = refs
    if not first:
        d_out, *refs = refs
    if not last:
        (field_out,) = refs
    total_m = cos_ref.shape[0]
    slots = d_ref.shape[0]
    groups = total_m // slots
    tiles = [received_tile(recv_ref, m, k, sections, slots) for m in range(slots) for k in range(groups // ROWS)]
    field = jnp.concatenate(tiles, axis=0)
    scalars = received_scalars(recv_ref, slots)
    rr_out[...] = scalars
    if not first:
        lane_ratio = scalars / rr_ref[...]
        ratio = unspread(lane_ratio)
        field = field + lane_ratio * field_ref[...]
    if not last:
        field_out[...] = field
    half = LANES // 2
    cosine, sine = cos_ref[...], sin_ref[...]
    turned = field * cosine + pltpu.roll(field, half, 1) * sine
    modes = jnp.concatenate([turned[:, :half], turned[:, half:]], axis=0)
    high = modes.astype(bf16).astype(f32)
    both = jnp.concatenate([high, modes - high], axis=0).astype(bf16)
    count = qq_ref.shape[1]
    cycles = qq_ref.shape[0]
    top = 2 * total_m
    pieces = []
    for c in range(count // chunk):
        here = slice(c * chunk, (c + 1) * chunk)
        pixels = lax.dot_general(
            both, table_ref[:, here], (((0,), (0,)), ((), ())), preferred_element_type=f32
        )
        mask = mask_ref[:, here].astype(f32)
        nqq, nqu, nuu = mask * qq_ref[:, here], mask * qu_ref[:, here], mask * uu_ref[:, here]
        parts = []
        for b in range(2):
            q = pixels[2 * b * cycles : (2 * b + 1) * cycles]
            u = pixels[(2 * b + 1) * cycles : (2 * b + 2) * cycles]
            parts += [nqq * q + nqu * u, nqu * q + nuu * u]
        pieces.append(jnp.concatenate(parts, axis=0).astype(bf16))
    weighted = jnp.concatenate(pieces, axis=1)
    folded = lax.dot_general(
        table_ref[:top, :], weighted, (((1,), (1,)), ((), ())), preferred_element_type=f32
    )
    folded = jnp.concatenate([folded[:total_m], folded[total_m:]], axis=1)
    out = folded * cosine - pltpu.roll(folded, half, 1) * sine
    curve = jnp.sum(field * out, axis=0, keepdims=True)
    first_side = (lane_index(curve.shape) // (half // 2)) % 2 == 0
    curve = join_halves(jnp.where(first_side, curve, 0.0), jnp.where(first_side, 0.0, curve))
    for m in range(slots):
        for k in range(groups // ROWS):
            at = (m * (groups // ROWS) + k) * ROWS
            send_tile(send_ref, out[at : at + ROWS], m, k, sections, slots)

    prior = prior_rows(prior_ref)
    own = None
    for m in range(slots):
        d = d_ref[m]
        if not first:
            d = r_ref[m] + by_row(ratio, (ROWS, LANES))[:, :1] * d
            d_out[m] = d
        product = prior * d * d
        own = product if own is None else own + product

    if first:
        for m in range(slots):
            turned_ref[m] = legendre_ref[m].T
    send_scalars(send_ref, curve + row_totals(own), slots)


def prior_rows(prior_ref):
    e = prior_ref[0:1, :]
    b = prior_ref[1:2, :]
    shape = (ROWS, prior_ref.shape[1])
    return jnp.where((row_index(shape) >> 1) & 1 == 0, jnp.broadcast_to(e, shape), jnp.broadcast_to(b, shape))


def image_terms(recv_ref, buffer_ref, m, sections, cycles, slots):
    tiles = []
    for k in range(cycles // LANES):
        at = m * (cycles // LANES) + k
        tile = received_tile(recv_ref, m, k, sections, slots)
        tiles.append(to_rows(tile, buffer_ref.at[at]))
    field = jnp.concatenate(tiles, axis=1) if len(tiles) > 1 else tiles[0]
    return split_rows(jnp.concatenate([-field, flip_signed(field)], axis=1))


def next_residual(both, legendre_ref, r_ref, d_ref, m, alpha, prior):
    image = jnp.dot(both, legendre_ref[m], preferred_element_type=f32)
    image = (image[:ROWS] + image[ROWS:]) + prior * d_ref[m]
    return r_ref[m] - alpha * image


def step_size(recv_ref, rr_ref, slots):
    curve = pair(received_scalars(recv_ref, slots))
    two = tuple(a / b for a, b in zip(unspread(rr_ref[...]), curve))
    return by_row(two, (ROWS, LANES))[:, :1]


def update_kernel(
    sections, cycles, first, recv_ref, rr_ref, prior_ref, legendre_ref, r_ref, d_ref, turned_ref, *refs
):
    if not first:
        x_ref, *refs = refs
    send_ref, r_out, x_out, buffer_ref = refs
    slots = r_ref.shape[0]
    alpha = step_size(recv_ref, rr_ref, slots)
    prior = prior_rows(prior_ref)
    square = None
    terms = [image_terms(recv_ref, buffer_ref, m, sections, cycles, slots) for m in range(slots)]
    waiting = None
    for m in range(slots + 1):
        if m < slots:
            r = next_residual(terms[m], legendre_ref, r_ref, d_ref, m, alpha, prior)
            r_out[m] = r
            square = r * r if square is None else square + r * r
            x_out[m] = alpha * d_ref[m] if first else x_ref[m] + alpha * d_ref[m]
        if waiting is not None:
            forward_send(turned_product(waiting, turned_ref, m - 1), send_ref, buffer_ref, m - 1, sections, cycles, slots)
        waiting = r
    send_scalars(send_ref, spread(pair(row_totals(square))), slots)


def last_kernel(
    sections,
    cycles,
    recv_ref,
    rr_ref,
    prior_ref,
    legendre_ref,
    r_ref,
    d_ref,
    x_ref,
    solution_ref,
    send_ref,
    residual_out,
    solution_out,
    buffer_ref,
):
    slots = r_ref.shape[0]
    alpha = step_size(recv_ref, rr_ref, slots)
    prior = prior_rows(prior_ref)
    for m in range(slots):
        x = x_ref[m] + alpha * d_ref[m]
        for b in range(2):
            solution_out[b, m] = solution_ref[b, m] + x[4 * b : 4 * b + 4]
    square = None
    terms = [image_terms(recv_ref, buffer_ref, m, sections, cycles, slots) for m in range(slots)]
    for m in range(slots):
        r = next_residual(terms[m], legendre_ref, r_ref, d_ref, m, alpha, prior)
        square = r * r if square is None else square + r * r
        for b in range(2):
            residual_out[b, m] = r[4 * b : 4 * b + 4]
    send_scalars(send_ref, row_totals(square), 0)


def end_kernel(
    recv_ref, rr_ref, d_ref, residual_ref, solution_ref, direction_hbm, residual_hbm, solution_hbm, direction_ref, sems
):
    slots = d_ref.shape[0]
    copies = [
        pltpu.make_async_copy(residual_ref, residual_hbm, sems.at[0]),
        pltpu.make_async_copy(solution_ref, solution_hbm, sems.at[1]),
        pltpu.make_async_copy(direction_ref, direction_hbm, sems.at[2]),
    ]
    copies[0].start()
    copies[1].start()
    before = unspread(rr_ref[...])
    now = pair(received_scalars(recv_ref, 0))
    ratios = [now[b] / before[b] for b in range(2)]

    def fill(m, carry):
        for b in range(2):
            direction_ref[b, m] = residual_ref[b, m] + ratios[b] * d_ref[m, 4 * b : 4 * b + 4]
        return carry

    lax.fori_loop(0, slots, fill, 0)
    copies[2].start()
    for copy in copies:
        copy.wait()


def call(kernel, outs, name, limit=24 << 20, hbm=(), scratch=(), hbm_outs=()):
    def run(*args):
        vmem = pl.BlockSpec(memory_space=pltpu.VMEM)
        specs = [vmem] * len(args)
        args = list(args)
        for i in hbm:
            specs[i] = pl.BlockSpec(memory_space=pltpu.HBM)
            args[i] = pltpu.with_memory_space_constraint(args[i], pltpu.HBM)
        return pl.pallas_call(
            kernel,
            out_shape=[jax.ShapeDtypeStruct(shape, dtype) for shape, dtype in outs],
            in_specs=specs,
            out_specs=[pl.BlockSpec(memory_space=pltpu.HBM) if i in hbm_outs else vmem for i in range(len(outs))],
            scratch_shapes=list(scratch),
            compiler_params=pltpu.CompilerParams(vmem_limit_bytes=limit),
            name=name,
        )(*args)

    return run


def per_device(
    solution_in,
    residual_in,
    direction_in,
    legendre,
    inverse_prior,
    noise_qq,
    noise_qu,
    noise_uu,
    pixel_mask,
    cycle_phase,
    m_values,
):
    sections = lax.axis_size("sec")
    devices = sections * lax.axis_size("grp")
    slots, cycles, length = legendre.shape[0], legendre.shape[2], legendre.shape[3]
    total_m = m_values.shape[0]
    count = noise_qq.shape[1]
    message = ((devices * (slots + 1), LANES), f32)
    scalars = ((devices, LANES), f32)
    inner = ((slots, ROWS, length), f32)
    outer = (solution_in.shape, f32)
    vector = ((1, LANES), f32)
    field_like = ((total_m, LANES), f32)
    chunk = min(256, count)

    buffers = (pltpu.VMEM((slots * (cycles // LANES), 10 * ROWS, LANES), f32),)

    def exchange(x):
        blocks = x.reshape(devices, 1, x.size // devices)
        return lax.all_to_all(blocks, ("sec", "grp"), 0, 0, tiled=True).reshape(x.shape)

    table = ((4 * total_m, count), bf16)
    blocks = ((slots, 2 * cycles, length), bf16)
    turned_blocks = ((slots, length, 2 * cycles), bf16)
    send, trig, cosine, sine, rows, r, d = call(
        functools.partial(start_kernel, sections, cycles),
        [message, table, field_like, field_like, blocks, inner, inner],
        "start",
        hbm=range(5),
        scratch=(
            pltpu.SMEM((total_m,), jnp.int32),
            pltpu.VMEM((cycle_phase.shape[0] // LANES, LANES), f32),
            pltpu.VMEM(residual_in.shape, f32),
            pltpu.VMEM(direction_in.shape, f32),
            *buffers,
            pltpu.SemaphoreType.DMA((2,)),
            pltpu.SemaphoreType.DMA((2,)),
            pltpu.SemaphoreType.DMA((slots,)),
        ),
    )(m_values, cycle_phase.reshape(-1, LANES), residual_in, direction_in, legendre.reshape(blocks[0]))
    noise = (noise_qq, noise_qu, noise_uu, pixel_mask)
    for step in range(ITERS):
        first, last = step == 0, step == ITERS - 1
        recv = exchange(send)
        carried = (rows,) if first else (r, field, rr)
        out = call(
            functools.partial(pixel_kernel, sections, chunk, first, last),
            [message, vector] + [turned_blocks if first else inner] + ([] if last else [field_like]),
            "pixels",
        )(recv, trig, cosine, sine, *noise, inverse_prior, d, *carried)
        send, rr, *out = out
        if first:
            turned, *out = out
        else:
            d, *out = out
        if not last:
            (field,) = out
        recv = exchange(send)
        carried = (recv, rr, inverse_prior, rows, r, d) + (() if last else (turned,)) + (() if first else (x,))
        if last:
            send, residual, solution = call(
                functools.partial(last_kernel, sections, cycles),
                [scalars, outer, outer],
                "last",
                scratch=buffers,
            )(*carried, solution_in)
        else:
            send, r, x = call(
                functools.partial(update_kernel, sections, cycles, first), [message, inner, inner], "update", scratch=buffers
            )(*carried)
    recv = exchange(send)
    direction, residual, solution = call(
        end_kernel,
        [outer, outer, outer],
        "end",
        hbm_outs=(0, 1, 2),
        scratch=(pltpu.VMEM(outer[0], f32), pltpu.SemaphoreType.DMA((3,))),
    )(recv, rr, d, residual, solution)
    return solution, residual, direction


def solution(mesh):
    return jax.shard_map(
        per_device,
        mesh=mesh,
        in_specs=(
            P(None, "grp", None, "sec"),
            P(None, "grp", None, "sec"),
            P(None, "grp", None, "sec"),
            P("grp", None, None, "sec"),
            P(None, "sec"),
            P("grp", "sec"),
            P("grp", "sec"),
            P("grp", "sec"),
            P("grp", "sec"),
            P(),
            P(),
        ),
        out_specs=(
            P(None, "grp", None, "sec"),
            P(None, "grp", None, "sec"),
            P(None, "grp", None, "sec"),
        ),
        check_vma=False,
    )
```

```python
import functools
import math

import jax
import jax.numpy as jnp
from jax import lax
from jax.experimental import pallas as pl
from jax.experimental.pallas import tpu as pltpu
from jax.sharding import PartitionSpec as P

ITERS = 4
LANES = 128
ROWS = 8
full_turn = 2.0 * math.pi
f32 = jnp.float32
bf16 = jnp.bfloat16

flipped = tuple(n ^ 3 for n in range(ROWS))


def row_index(shape):
    return lax.broadcasted_iota(jnp.int32, shape, 0)


def lane_index(shape):
    return lax.broadcasted_iota(jnp.int32, shape, 1)


def permute_rows(x, order):
    rows = row_index(x.shape)
    by_shift = {}
    for t, n in enumerate(order):
        by_shift.setdefault((t - n) % ROWS, []).append(t)
    out = None
    for shift, targets in by_shift.items():
        moved = pltpu.roll(x, shift, 0) if shift else x
        if out is None:
            out = moved
        else:
            mask = functools.reduce(jnp.logical_or, [rows == t for t in targets])
            out = jnp.where(mask, moved, out)
    return out


def turn_blocks(buffer_ref, start, stride, distance):
    width = LANES // ROWS
    out = None
    for k in range(ROWS):
        moved = buffer_ref[pl.ds(start + 4 * k, ROWS, stride=stride), :]
        out = moved if out is None else jnp.where(distance == k, pltpu.roll(moved, k * width, 1), out)
    return out


def store_copies(x, buffer_ref, starts, stride):
    for start in starts:
        buffer_ref[pl.ds(start, ROWS, stride=stride), :] = x


def to_rows(x, buffer_ref):
    store_copies(x, buffer_ref, (16, 48, 2, 34), 4)
    rows = row_index(x.shape)
    place = (rows & 1) * 4 + (rows >> 1)
    distance = (lane_index(x.shape) // (LANES // ROWS) - place) & (ROWS - 1)
    return turn_blocks(buffer_ref, 16, 2, distance)


def to_message(x, buffer_ref):
    store_copies(x, buffer_ref, (0, 14, 32, 46), 2)
    distance = (lane_index(x.shape) // (LANES // ROWS) - row_index(x.shape)) & (ROWS - 1)
    return turn_blocks(buffer_ref, 0, 4, distance)


def split_rows(x):
    high = x.astype(bf16).astype(f32)
    return jnp.concatenate([high, x - high], axis=0).astype(bf16)


def flip_signed(x):
    rows = row_index(x.shape)
    same = ((rows >> 1) & 1) == (rows & 1)
    moved = permute_rows(x, flipped)
    return jnp.where(same, moved, -moved)


def row_totals(x):
    tile = x[:, :LANES]
    for k in range(1, x.shape[1] // LANES):
        tile = tile + x[:, k * LANES : (k + 1) * LANES]
    rows = row_index(tile.shape)
    first = jnp.sum(jnp.where(rows < 4, tile, 0.0), axis=0, keepdims=True)
    second = jnp.sum(jnp.where(rows < 4, 0.0, tile), axis=0, keepdims=True)
    return join_halves(first, second)


def join_halves(first, second):
    first = first + pltpu.roll(first, LANES // 2, 1)
    second = second + pltpu.roll(second, LANES // 2, 1)
    return jnp.where(lane_index(first.shape) < LANES // 2, first, second)


def pair(vector):
    low = lane_index(vector.shape) < LANES // 2
    return (
        jnp.sum(jnp.where(low, vector, 0.0), axis=1, keepdims=True),
        jnp.sum(jnp.where(low, 0.0, vector), axis=1, keepdims=True),
    )


def spread(two):
    return by_lane(two, (1, LANES))


def unspread(vector):
    spot = lane_index(vector.shape)
    return [jnp.sum(jnp.where(spot == b * (LANES // 4), vector, 0.0), axis=1, keepdims=True) for b in range(2)]


def by_row(two, shape):
    return jnp.where(row_index(shape) < 4, two[0], two[1])


def by_lane(two, shape):
    quarter = LANES // 4
    return jnp.where((lane_index(shape) // quarter) % 2 == 0, two[0], two[1])


def forward_product(values, legendre_ref, m):
    return lax.dot_general(
        split_rows(values),
        legendre_ref[m],
        (((1,), (1,)), ((), ())),
        preferred_element_type=f32,
    )


def turned_product(values, turned_ref, m):
    return jnp.dot(split_rows(values), turned_ref[m], preferred_element_type=f32)


def forward_send(prod, send_ref, buffer_ref, m, sections, cycles, slots):
    prod = prod[:ROWS] + prod[ROWS:]
    field = flip_signed(prod[:, cycles:]) - prod[:, :cycles]
    for k in range(cycles // LANES):
        tile = field[:, k * LANES : (k + 1) * LANES]
        at = m * (cycles // LANES) + k
        send_tile(send_ref, to_message(tile, buffer_ref.at[at]), m, k, sections, slots)


def tile_rows(ref, m, k, s, sections, slots):
    groups = ref.shape[0] // (slots + 1) // sections
    return pl.ds((s * groups + k * ROWS) * (slots + 1) + m, ROWS, stride=slots + 1)


def send_tile(send_ref, tile, m, k, sections, slots):
    for s in range(sections):
        send_ref[tile_rows(send_ref, m, k, s, sections, slots), :] = tile


def scalar_rows(ref, slots):
    count = ref.shape[0] // (slots + 1)
    return pl.ds(slots, count, stride=slots + 1) if slots else slice(None)


def send_scalars(send_ref, vector, slots):
    count = send_ref.shape[0] // (slots + 1)
    send_ref[scalar_rows(send_ref, slots), :] = jnp.broadcast_to(vector, (count, LANES))


def received_scalars(recv_ref, slots):
    return jnp.sum(recv_ref[scalar_rows(recv_ref, slots), :], axis=0, keepdims=True)


def received_tile(recv_ref, m, k, sections, slots):
    total = None
    for s in range(sections):
        part = recv_ref[tile_rows(recv_ref, m, k, s, sections, slots), :]
        total = part if total is None else total + part
    return total


def fill_tables(slots, total, m_ref, phase_ref, table_ref, cos_ref, sin_ref):
    total_m = cos_ref.shape[0]
    count = table_ref.shape[1]
    groups = total_m // slots
    rows = row_index((ROWS, LANES))
    columns = []
    for m in range(slots):
        for k in range(groups // ROWS):
            column = jnp.zeros((ROWS, LANES), jnp.int32)
            for i in range(ROWS):
                column = jnp.where(rows == i, m_ref[(k * ROWS + i) * slots + m], column)
            columns.append(column)
    column = jnp.concatenate(columns, axis=0)
    value = column.astype(f32)
    weight = jnp.where(column == 0, 1.0, 2.0).astype(f32)
    lanes = lane_index(column.shape)

    me = lax.axis_index("grp")
    width = LANES // ROWS
    phases = phase_ref[pl.ds(me // ROWS, 1), :]
    spot = lane_index(phases.shape)
    moved = pltpu.roll(phases, (ROWS - me % ROWS) % ROWS * width, 1)
    local = jnp.where(spot < width, moved, 0.0)
    for k in (1, 2, 4):
        local = local + pltpu.roll(local, k * width, 1)
    turn = value * local
    cosine = jnp.cos(turn)
    sine = jnp.sin(turn)
    cos_ref[...] = cosine
    sin_ref[...] = jnp.where(lanes < LANES // 2, -sine, sine)

    def wrap(index):
        return index & (total - 1) if total & (total - 1) == 0 else index % total

    step = full_turn / total
    start = lax.axis_index("sec") * count
    fine = wrap(column * lanes).astype(f32) * step
    coarse = wrap(column * (start + lanes * LANES)).astype(f32) * step
    fine_cos, fine_sin = jnp.cos(fine), jnp.sin(fine)
    coarse_cos, coarse_sin = weight * jnp.cos(coarse), weight * jnp.sin(coarse)
    for a in range(count // LANES):
        cos_a = coarse_cos[:, a : a + 1]
        sin_a = coarse_sin[:, a : a + 1]
        block = jnp.concatenate([cos_a * fine_cos - sin_a * fine_sin, -(sin_a * fine_cos + cos_a * fine_sin)], axis=0)
        block = block.astype(bf16)
        here = slice(a * LANES, (a + 1) * LANES)
        table_ref[: 2 * total_m, here] = block
        table_ref[2 * total_m :, here] = block


def start_kernel(
    sections,
    cycles,
    m_hbm,
    phase_hbm,
    residual_hbm,
    direction_hbm,
    legendre_hbm,
    send_ref,
    table_ref,
    cos_ref,
    sin_ref,
    legendre_ref,
    r_ref,
    d_ref,
    m_ref,
    phase_ref,
    residual_ref,
    direction_ref,
    buffer_ref,
    small_sems,
    value_sems,
    legendre_sems,
):
    slots = r_ref.shape[0]
    small = [
        pltpu.make_async_copy(m_hbm, m_ref, small_sems.at[0]),
        pltpu.make_async_copy(phase_hbm, phase_ref, small_sems.at[1]),
    ]
    for copy in small:
        copy.start()
    copies = [
        pltpu.make_async_copy(direction_hbm, direction_ref, value_sems.at[0]),
        pltpu.make_async_copy(residual_hbm, residual_ref, value_sems.at[1]),
    ]
    blocks = [
        pltpu.make_async_copy(legendre_hbm.at[m], legendre_ref.at[m], legendre_sems.at[m]) for m in range(slots)
    ]
    for copy in copies:
        copy.start()
    for block in blocks:
        block.start()
    for copy in small:
        copy.wait()
    fill_tables(slots, table_ref.shape[1] * sections, m_ref, phase_ref, table_ref, cos_ref, sin_ref)
    copies[0].wait()
    rows = []
    for m in range(slots):
        d = jnp.concatenate([direction_ref[0, m], direction_ref[1, m]], axis=0)
        d_ref[m] = d
        rows.append(d)
    copies[1].wait()
    square = None
    for m in range(slots):
        r = jnp.concatenate([residual_ref[0, m], residual_ref[1, m]], axis=0)
        r_ref[m] = r
        square = r * r if square is None else square + r * r
    send_scalars(send_ref, spread(pair(row_totals(square))), slots)
    for block in blocks:
        block.wait()
    for m in range(slots):
        forward_send(forward_product(rows[m], legendre_ref, m), send_ref, buffer_ref, m, sections, cycles, slots)


def pixel_kernel(
    sections,
    chunk,
    first,
    last,
    recv_ref,
    table_ref,
    cos_ref,
    sin_ref,
    qq_ref,
    qu_ref,
    uu_ref,
    prior_ref,
    d_ref,
    *refs,
):
    if first:
        mask_ref, legendre_ref, *refs = refs
    else:
        r_ref, field_ref, rr_ref, *refs = refs
    send_ref, rr_out, *refs = refs
    if first:
        turned_ref, *refs, nqq_out, nqu_out, nuu_out = refs
    if not first:
        d_out, *refs = refs
    if not last:
        (field_out,) = refs
    total_m = cos_ref.shape[0]
    slots = d_ref.shape[0]
    groups = total_m // slots
    tiles = [received_tile(recv_ref, m, k, sections, slots) for m in range(slots) for k in range(groups // ROWS)]
    field = jnp.concatenate(tiles, axis=0)
    scalars = received_scalars(recv_ref, slots)
    rr_out[...] = scalars
    if not first:
        lane_ratio = scalars / rr_ref[...]
        ratio = unspread(lane_ratio)
        field = field + lane_ratio * field_ref[...]
    if not last:
        field_out[...] = field
    half = LANES // 2
    cosine, sine = cos_ref[...], sin_ref[...]
    turned = field * cosine + pltpu.roll(field, half, 1) * sine
    modes = jnp.concatenate([turned[:, :half], turned[:, half:]], axis=0)
    high = modes.astype(bf16).astype(f32)
    both = jnp.concatenate([high, modes - high], axis=0).astype(bf16)
    count = qq_ref.shape[1]
    cycles = qq_ref.shape[0]
    top = 2 * total_m
    pieces = []
    for c in range(count // chunk):
        here = slice(c * chunk, (c + 1) * chunk)
        pixels = lax.dot_general(
            both, table_ref[:, here], (((0,), (0,)), ((), ())), preferred_element_type=f32
        )
        nqq, nqu, nuu = qq_ref[:, here], qu_ref[:, here], uu_ref[:, here]
        if first:
            mask = mask_ref[:, here].astype(f32)
            nqq, nqu, nuu = mask * nqq, mask * nqu, mask * nuu
            nqq_out[:, here], nqu_out[:, here], nuu_out[:, here] = nqq, nqu, nuu
        parts = []
        for b in range(2):
            q = pixels[2 * b * cycles : (2 * b + 1) * cycles]
            u = pixels[(2 * b + 1) * cycles : (2 * b + 2) * cycles]
            parts += [nqq * q + nqu * u, nqu * q + nuu * u]
        pieces.append(jnp.concatenate(parts, axis=0).astype(bf16))
    weighted = jnp.concatenate(pieces, axis=1)
    folded = lax.dot_general(
        table_ref[:top, :], weighted, (((1,), (1,)), ((), ())), preferred_element_type=f32
    )
    folded = jnp.concatenate([folded[:total_m], folded[total_m:]], axis=1)
    out = folded * cosine - pltpu.roll(folded, half, 1) * sine
    curve = jnp.sum(field * out, axis=0, keepdims=True)
    first_side = (lane_index(curve.shape) // (half // 2)) % 2 == 0
    curve = join_halves(jnp.where(first_side, curve, 0.0), jnp.where(first_side, 0.0, curve))
    for m in range(slots):
        for k in range(groups // ROWS):
            at = (m * (groups // ROWS) + k) * ROWS
            send_tile(send_ref, out[at : at + ROWS], m, k, sections, slots)

    prior = prior_rows(prior_ref)
    own = None
    for m in range(slots):
        d = d_ref[m]
        if not first:
            d = r_ref[m] + by_row(ratio, (ROWS, LANES))[:, :1] * d
            d_out[m] = d
        product = prior * d * d
        own = product if own is None else own + product

    if first:
        for m in range(slots):
            turned_ref[m] = legendre_ref[m].T
    send_scalars(send_ref, curve + row_totals(own), slots)


def prior_rows(prior_ref):
    e = prior_ref[0:1, :]
    b = prior_ref[1:2, :]
    shape = (ROWS, prior_ref.shape[1])
    return jnp.where((row_index(shape) >> 1) & 1 == 0, jnp.broadcast_to(e, shape), jnp.broadcast_to(b, shape))


def image_terms(recv_ref, buffer_ref, m, sections, cycles, slots):
    tiles = []
    for k in range(cycles // LANES):
        at = m * (cycles // LANES) + k
        tile = received_tile(recv_ref, m, k, sections, slots)
        tiles.append(to_rows(tile, buffer_ref.at[at]))
    field = jnp.concatenate(tiles, axis=1) if len(tiles) > 1 else tiles[0]
    return split_rows(jnp.concatenate([-field, flip_signed(field)], axis=1))


def next_residual(both, legendre_ref, r_ref, d_ref, m, alpha, prior):
    image = jnp.dot(both, legendre_ref[m], preferred_element_type=f32)
    image = (image[:ROWS] + image[ROWS:]) + prior * d_ref[m]
    return r_ref[m] - alpha * image


def step_size(recv_ref, rr_ref, slots):
    curve = pair(received_scalars(recv_ref, slots))
    two = tuple(a / b for a, b in zip(unspread(rr_ref[...]), curve))
    return by_row(two, (ROWS, LANES))[:, :1]


def update_kernel(
    sections, cycles, first, recv_ref, rr_ref, prior_ref, legendre_ref, r_ref, d_ref, turned_ref, *refs
):
    if not first:
        x_ref, *refs = refs
    send_ref, r_out, x_out, buffer_ref = refs
    slots = r_ref.shape[0]
    alpha = step_size(recv_ref, rr_ref, slots)
    prior = prior_rows(prior_ref)
    square = None
    terms = [image_terms(recv_ref, buffer_ref, m, sections, cycles, slots) for m in range(slots)]
    waiting = None
    for m in range(slots + 1):
        if m < slots:
            r = next_residual(terms[m], legendre_ref, r_ref, d_ref, m, alpha, prior)
            r_out[m] = r
            square = r * r if square is None else square + r * r
            x_out[m] = alpha * d_ref[m] if first else x_ref[m] + alpha * d_ref[m]
        if waiting is not None:
            forward_send(turned_product(waiting, turned_ref, m - 1), send_ref, buffer_ref, m - 1, sections, cycles, slots)
        waiting = r
    send_scalars(send_ref, spread(pair(row_totals(square))), slots)


def last_kernel(
    sections,
    cycles,
    recv_ref,
    rr_ref,
    prior_ref,
    legendre_ref,
    r_ref,
    d_ref,
    x_ref,
    solution_ref,
    send_ref,
    residual_out,
    solution_out,
    buffer_ref,
):
    slots = r_ref.shape[0]
    alpha = step_size(recv_ref, rr_ref, slots)
    prior = prior_rows(prior_ref)
    for m in range(slots):
        x = x_ref[m] + alpha * d_ref[m]
        for b in range(2):
            solution_out[b, m] = solution_ref[b, m] + x[4 * b : 4 * b + 4]
    square = None
    terms = [image_terms(recv_ref, buffer_ref, m, sections, cycles, slots) for m in range(slots)]
    for m in range(slots):
        r = next_residual(terms[m], legendre_ref, r_ref, d_ref, m, alpha, prior)
        square = r * r if square is None else square + r * r
        for b in range(2):
            residual_out[b, m] = r[4 * b : 4 * b + 4]
    send_scalars(send_ref, row_totals(square), 0)


def end_kernel(
    recv_ref, rr_ref, d_ref, residual_ref, solution_ref, direction_hbm, residual_hbm, solution_hbm, direction_ref, sems
):
    slots = d_ref.shape[0]
    copies = [
        pltpu.make_async_copy(residual_ref, residual_hbm, sems.at[0]),
        pltpu.make_async_copy(solution_ref, solution_hbm, sems.at[1]),
        pltpu.make_async_copy(direction_ref, direction_hbm, sems.at[2]),
    ]
    copies[0].start()
    copies[1].start()
    before = unspread(rr_ref[...])
    now = pair(received_scalars(recv_ref, 0))
    ratios = [now[b] / before[b] for b in range(2)]

    def fill(m, carry):
        for b in range(2):
            direction_ref[b, m] = residual_ref[b, m] + ratios[b] * d_ref[m, 4 * b : 4 * b + 4]
        return carry

    lax.fori_loop(0, slots, fill, 0)
    copies[2].start()
    for copy in copies:
        copy.wait()


def call(kernel, outs, name, limit=24 << 20, hbm=(), scratch=(), hbm_outs=()):
    def run(*args):
        vmem = pl.BlockSpec(memory_space=pltpu.VMEM)
        specs = [vmem] * len(args)
        args = list(args)
        for i in hbm:
            specs[i] = pl.BlockSpec(memory_space=pltpu.HBM)
            args[i] = pltpu.with_memory_space_constraint(args[i], pltpu.HBM)
        return pl.pallas_call(
            kernel,
            out_shape=[jax.ShapeDtypeStruct(shape, dtype) for shape, dtype in outs],
            in_specs=specs,
            out_specs=[pl.BlockSpec(memory_space=pltpu.HBM) if i in hbm_outs else vmem for i in range(len(outs))],
            scratch_shapes=list(scratch),
            compiler_params=pltpu.CompilerParams(vmem_limit_bytes=limit),
            name=name,
        )(*args)

    return run


def per_device(
    solution_in,
    residual_in,
    direction_in,
    legendre,
    inverse_prior,
    noise_qq,
    noise_qu,
    noise_uu,
    pixel_mask,
    cycle_phase,
    m_values,
):
    sections = lax.axis_size("sec")
    devices = sections * lax.axis_size("grp")
    slots, cycles, length = legendre.shape[0], legendre.shape[2], legendre.shape[3]
    total_m = m_values.shape[0]
    count = noise_qq.shape[1]
    message = ((devices * (slots + 1), LANES), f32)
    scalars = ((devices, LANES), f32)
    inner = ((slots, ROWS, length), f32)
    outer = (solution_in.shape, f32)
    vector = ((1, LANES), f32)
    field_like = ((total_m, LANES), f32)
    chunk = min(256, count)

    buffers = (pltpu.VMEM((slots * (cycles // LANES), 10 * ROWS, LANES), f32),)

    def exchange(x):
        blocks = x.reshape(devices, 1, x.size // devices)
        return lax.all_to_all(blocks, ("sec", "grp"), 0, 0, tiled=True).reshape(x.shape)

    table = ((4 * total_m, count), bf16)
    blocks = ((slots, 2 * cycles, length), bf16)
    turned_blocks = ((slots, length, 2 * cycles), bf16)
    send, trig, cosine, sine, rows, r, d = call(
        functools.partial(start_kernel, sections, cycles),
        [message, table, field_like, field_like, blocks, inner, inner],
        "start",
        hbm=range(5),
        scratch=(
            pltpu.SMEM((total_m,), jnp.int32),
            pltpu.VMEM((cycle_phase.shape[0] // LANES, LANES), f32),
            pltpu.VMEM(residual_in.shape, f32),
            pltpu.VMEM(direction_in.shape, f32),
            *buffers,
            pltpu.SemaphoreType.DMA((2,)),
            pltpu.SemaphoreType.DMA((2,)),
            pltpu.SemaphoreType.DMA((slots,)),
        ),
    )(m_values, cycle_phase.reshape(-1, LANES), residual_in, direction_in, legendre.reshape(blocks[0]))
    noise = (noise_qq, noise_qu, noise_uu)
    for step in range(ITERS):
        first, last = step == 0, step == ITERS - 1
        recv = exchange(send)
        carried = (pixel_mask, rows) if first else (r, field, rr)
        out = call(
            functools.partial(pixel_kernel, sections, chunk, first, last),
            [message, vector] + [turned_blocks if first else inner] + ([] if last else [field_like]) + [(noise_qq.shape, f32)] * (3 if first else 0),
            "pixels",
        )(recv, trig, cosine, sine, *noise, inverse_prior, d, *carried)
        send, rr, *out = out
        if first:
            turned, *out = out
            *out, nqq, nqu, nuu = out
            noise = (nqq, nqu, nuu)
        else:
            d, *out = out
        if not last:
            (field,) = out
        recv = exchange(send)
        carried = (recv, rr, inverse_prior, rows, r, d) + (() if last else (turned,)) + (() if first else (x,))
        if last:
            send, residual, solution = call(
                functools.partial(last_kernel, sections, cycles),
                [scalars, outer, outer],
                "last",
                scratch=buffers,
            )(*carried, solution_in)
        else:
            send, r, x = call(
                functools.partial(update_kernel, sections, cycles, first), [message, inner, inner], "update", scratch=buffers
            )(*carried)
    recv = exchange(send)
    direction, residual, solution = call(
        end_kernel,
        [outer, outer, outer],
        "end",
        hbm_outs=(0, 1, 2),
        scratch=(pltpu.VMEM(outer[0], f32), pltpu.SemaphoreType.DMA((3,))),
    )(recv, rr, d, residual, solution)
    return solution, residual, direction


def solution(mesh):
    return jax.shard_map(
        per_device,
        mesh=mesh,
        in_specs=(
            P(None, "grp", None, "sec"),
            P(None, "grp", None, "sec"),
            P(None, "grp", None, "sec"),
            P("grp", None, None, "sec"),
            P(None, "sec"),
            P("grp", "sec"),
            P("grp", "sec"),
            P("grp", "sec"),
            P("grp", "sec"),
            P(),
            P(),
        ),
        out_specs=(
            P(None, "grp", None, "sec"),
            P(None, "grp", None, "sec"),
            P(None, "grp", None, "sec"),
        ),
        check_vma=False,
    )
```
